128 devices in a mesh: freq: 4 (over x_hi, core), space: 32 (over z, y, x_lo).
Axes of the slice: x: 4 (x_hi: 2, x_lo: 2; x = x_hi * 2 + x_lo), y: 4, z: 4, core: 2. Of those that a mesh axis runs over, the one named last changes fastest.
Arguments:
- saved_modes: bfloat16 [4, 4, 2, 2, 3, 512, 128, 128], P('freq', None, None, None, None, 'space'), may hold values from -6 to 6
- mode_gains: float32 [4, 4], P('freq'), may hold values from 0.5 to 4
Outputs:
- smoothed_gradient: float32 [512, 128, 128], P('space', 'freq')
The draws below stay inside these ranges and needn't reach their ends.
All inputs are finite; a program needn't handle non-finite values.
Results may differ from the reference program's by a relative error of at most 0.0003.
Values may be sent and summed in bfloat16 or wider, within the bound.
A program may use at most 256 MiB of HBM per device.

```python
import math
import jax
import jax.numpy as jnp
from jax import lax

NY = 128
NZ = 128
MODES = 4
NX = 512
FREQS = 4


def block_scale(own_key, dims, pieces, least, largest):
    level, own = 1.0, jax.random.fold_in(own_key, 6)
    for position, shards_of in pieces:
        heights = jnp.exp(jax.random.uniform(jax.random.fold_in(own, position), (shards_of,), jnp.float32, least / len(pieces), largest / len(pieces)))
        level = level * jnp.repeat(heights, dims[position] // shards_of).reshape([-1 if axis == position else 1 for axis in range(len(dims))])
    return level


def scatter_about(own_key, extent, spread, reach, split=(), kind=jnp.bfloat16):
    entries = jax.random.normal(own_key, extent, jnp.float32) * spread
    if len(split) > 0:
        entries = block_scale(own_key, extent, split, -0.22, 0.18) * entries
    return jnp.clip(entries, min=-reach, max=reach).astype(kind)


def setup_inputs(seed: int = 0) -> dict:
    key_list = jax.random.split(jax.random.key(seed), 3)
    return {
        "saved_modes": scatter_about(key_list[0], (FREQS, MODES, 2, 2, 3, NX, NY, NZ), 1.0, 6.0, ((0, 4), (5, 32))),
        "mode_gains": jnp.clip(jnp.exp(math.log(4.0) - 2.0794415 * jax.random.uniform(key_list[1], (FREQS, MODES), jnp.float32) ** block_scale(key_list[1], (FREQS, MODES), ((0, 4),), -0.2, 0.2)), 0.5, 4.0),
    }


AXIAL = 0.35
CROSS = 0.06


def central_diffs(grid_values):
    padded = jnp.pad(grid_values, ((0, 0), (0, 0), (1, 1), (1, 1), (1, 1)))
    along_x = (padded[:, :, 2:, 1:-1, 1:-1] - padded[:, :, :-2, 1:-1, 1:-1]) * 0.5
    along_y = (padded[:, :, 1:-1, 2:, 1:-1] - padded[:, :, 1:-1, :-2, 1:-1]) * 0.5
    along_z = (padded[:, :, 1:-1, 1:-1, 2:] - padded[:, :, 1:-1, 1:-1, :-2]) * 0.5
    return (along_x, along_y, along_z)


def strain_dot(grad_forward, grad_adjoint):
    running = jnp.zeros(grad_forward[0].shape[2:], jnp.float32)
    for row_axis in range(3):
        for col_axis in range(3):
            strain_u = 0.5 * (grad_forward[row_axis][:, col_axis] + grad_forward[col_axis][:, row_axis])
            strain_v = 0.5 * (grad_adjoint[row_axis][:, col_axis] + grad_adjoint[col_axis][:, row_axis])
            running = running + jnp.sum(strain_u * strain_v, axis=0)
    return running


def smooth_pass(grid_values):
    padded = jnp.pad(grid_values, 1)
    center = grid_values
    axial = padded[2:, 1:-1, 1:-1] + padded[:-2, 1:-1, 1:-1] - 2.0 * center
    cross = padded[1:-1, 2:, 1:-1] + padded[1:-1, :-2, 1:-1] + padded[1:-1, 1:-1, 2:] + padded[1:-1, 1:-1, :-2] - 4.0 * center
    return center + AXIAL * axial + CROSS * cross


def reference(saved_modes, mode_gains):
    freq_total = saved_modes.shape[0]
    mode_count = saved_modes.shape[1]
    factor = -2.0 / (freq_total * mode_count)

    def one_pair(pair_index, running):
        freq_index = pair_index // mode_count
        mode_index = pair_index % mode_count
        mode_pair = lax.dynamic_index_in_dim(saved_modes, freq_index, 0, False)
        mode_pair = lax.dynamic_index_in_dim(mode_pair, mode_index, 0, False).astype(jnp.float32)
        weight = lax.dynamic_index_in_dim(lax.dynamic_index_in_dim(mode_gains, freq_index, 0, False), mode_index, 0, False)
        return running + (factor * weight) * strain_dot(central_diffs(mode_pair[0]), central_diffs(mode_pair[1]))

    sensitivity = lax.fori_loop(0, freq_total * mode_count, one_pair, jnp.zeros(saved_modes.shape[5:], jnp.float32))
    for sweep in range(3):
        sensitivity = smooth_pass(sensitivity)
    return sensitivity
```

```python
import functools

import jax
import jax.numpy as jnp
from jax import lax
from jax.experimental import pallas as pl
from jax.experimental.pallas import tpu as pltpu
from jax.sharding import PartitionSpec as P

AXIAL = 0.35
CROSS = 0.06


def padded_2(block, sides, width):
    for axis, dim in sides:
        count = lax.axis_size(axis)
        forward = [(i, i + 1) for i in range(count - 1)]
        backward = [(target, source) for source, target in forward]
        low = lax.ppermute(
            lax.slice_in_dim(block, block.shape[dim] - width, None, axis=dim), axis, forward
        )
        high = lax.ppermute(lax.slice_in_dim(block, 0, width, axis=dim), axis, backward)
        block = jnp.concatenate([low, block, high], axis=dim)
    return block


def split_up(x, dim, size):
    dims = x.shape
    tiles = x.reshape(*dims[:dim], size, dims[dim] // size, *dims[dim + 1 :])
    return jnp.moveaxis(tiles, dim, 0)


def sum_at_owner(x, axis, dim):
    tiles = split_up(x, dim, lax.axis_size(axis))
    arrived = lax.all_to_all(tiles, axis, split_axis=0, concat_axis=0, tiled=True)
    return arrived.sum(axis=0)


def shift_z(grid_values, upward):
    zero_plane = jnp.zeros(grid_values.shape[:-1] + (1,), grid_values.dtype)
    if upward:
        return jnp.concatenate([grid_values[..., 1:], zero_plane], axis=-1)
    return jnp.concatenate([zero_plane, grid_values[..., :-1]], axis=-1)

MESH = pl.DeviceIdType.MESH


def diff_matrices(count):
    row = lax.broadcasted_iota(jnp.int32, (count, count), 0)
    col = lax.broadcasted_iota(jnp.int32, (count, count), 1)
    upper = (col == row + 1).astype(jnp.float32)
    lower = (col + 1 == row).astype(jnp.float32)
    along_rows = (upper - lower).astype(jnp.bfloat16)
    along_cols = (lower - upper).astype(jnp.bfloat16)
    return along_rows, along_cols


def strain_parts(field, x, diff_y, diff_z, low, high):
    center = [field[c, x] for c in range(3)]
    after = [field[c, x + 1].astype(jnp.float32) for c in range(3)]
    before = [field[c, x - 1].astype(jnp.float32) for c in range(3)]
    if high is not None:
        after = [value * high for value in after]
    if low is not None:
        before = [value * low for value in before]
    dx = [after[c] - before[c] for c in range(3)]
    dy = [jnp.dot(diff_y, center[c], preferred_element_type=jnp.float32) for c in range(3)]
    dz = [jnp.dot(center[c], diff_z, preferred_element_type=jnp.float32) for c in range(3)]
    return (dx[0], dy[1], dz[2], dx[1] + dy[0], dx[2] + dz[0], dy[2] + dz[1])


def pair_term(forward, adjoint, x, diff_y, diff_z, low=None, high=None):
    eu = strain_parts(forward, x, diff_y, diff_z, low, high)
    ev = strain_parts(adjoint, x, diff_y, diff_z, low, high)
    straight = eu[0] * ev[0] + eu[1] * ev[1] + eu[2] * ev[2]
    shear = eu[3] * ev[3] + eu[4] * ev[4] + eu[5] * ev[5]
    return straight + 0.5 * shear


def strain_kernel(space, factor, modes, gains, out, buf, ymat, zmat, load_sem, send_sem, recv_sem):
    mode_count = modes.shape[1]
    planes = modes.shape[5]
    me = lax.axis_index("space")
    above = lax.rem(me + 1, space)
    below = lax.rem(me + space - 1, space)

    def load(m):
        return pltpu.make_async_copy(
            modes.at[0, m], buf.at[m, :, :, :, pl.ds(1, planes)], load_sem.at[m]
        )

    def halo(c, side):
        m, part = c // 2, lax.rem(c, 2)
        plane, slot, target = (planes - 1, 0, above) if side == 0 else (0, planes + 1, below)
        return pltpu.make_async_remote_copy(
            src_ref=modes.at[0, m, :, part, :, plane],
            dst_ref=buf.at[m, :, part, :, slot],
            send_sem=send_sem.at[side, c],
            recv_sem=recv_sem.at[side, c],
            device_id={"space": target},
            device_id_type=MESH,
        )

    load(0).start()
    barrier = pltpu.get_barrier_semaphore()
    for target in (above, below):
        pl.semaphore_signal(barrier, inc=1, device_id={"space": target}, device_id_type=MESH)
    pl.semaphore_wait(barrier, 2)

    @pl.loop(0, 2 * mode_count)
    def _(c):
        halo(c, 0).start()
        halo(c, 1).start()

    @pl.loop(1, mode_count)
    def _(m):
        load(m).start()

    diff_y, diff_z = diff_matrices(modes.shape[6])
    ymat[...] = diff_y
    zmat[...] = diff_z
    out[...] = jnp.zeros_like(out)

    def term(m, part, x, low=None, high=None):
        return pair_term(
            buf.at[m, 0, part], buf.at[m, 1, part], x, ymat[...], zmat[...], low, high
        )

    @pl.loop(0, mode_count)
    def _(m):
        load(m).wait()
        weight = gains[0, m] * (0.25 * factor)

        @pl.loop(2, planes)
        def _(x):
            out[x - 1] += weight * (term(m, 0, x) + term(m, 1, x))

    low = jnp.where(me > 0, 1.0, 0.0).astype(jnp.float32)
    high = jnp.where(me < space - 1, 1.0, 0.0).astype(jnp.float32)

    @pl.loop(0, 2 * mode_count)
    def _(c):
        m, part = c // 2, lax.rem(c, 2)
        weight = gains[0, m] * (0.25 * factor)
        halo(c, 0).wait_recv()
        out[0] += weight * term(m, part, 1, low=low)
        halo(c, 1).wait_recv()
        out[planes - 1] += weight * term(m, part, planes, high=high)

    @pl.loop(0, 2 * mode_count)
    def _(c):
        halo(c, 0).wait_send()
        halo(c, 1).wait_send()


def partial_sensitivity(saved_modes, mode_gains, factor):
    _, mode_count, pair, parts, comps, planes, rows, cols = saved_modes.shape
    return pl.pallas_call(
        functools.partial(strain_kernel, lax.axis_size("space"), factor),
        out_shape=jax.ShapeDtypeStruct((planes, rows, cols), jnp.float32),
        in_specs=[
            pl.BlockSpec(memory_space=pl.ANY),
            pl.BlockSpec(memory_space=pltpu.SMEM),
        ],
        out_specs=pl.BlockSpec(memory_space=pltpu.VMEM),
        scratch_shapes=[
            pltpu.VMEM((mode_count, pair, parts, comps, planes + 2, rows, cols), jnp.bfloat16),
            pltpu.VMEM((rows, rows), jnp.bfloat16),
            pltpu.VMEM((cols, cols), jnp.bfloat16),
            pltpu.SemaphoreType.DMA((mode_count,)),
            pltpu.SemaphoreType.DMA((2, 2 * mode_count)),
            pltpu.SemaphoreType.DMA((2, 2 * mode_count)),
        ],
        compiler_params=pltpu.CompilerParams(
            collective_id=0, has_side_effects=True, vmem_limit_bytes=60 << 20
        ),
    )(saved_modes, mode_gains)


def smooth_step(padded):
    center = padded[1:-1, 1:-1]
    axial = padded[2:, 1:-1] + padded[:-2, 1:-1] - 2.0 * center
    cross = (
        padded[1:-1, 2:]
        + padded[1:-1, :-2]
        + shift_z(center, True)
        + shift_z(center, False)
        - 4.0 * center
    )
    return center + AXIAL * axial + CROSS * cross


def deep_smooth(grid_values):
    slab_rows = grid_values.shape[0]
    band_rows = grid_values.shape[1]
    first_x = lax.axis_index("space") * slab_rows - 3
    total_x = slab_rows * lax.axis_size("space")
    padded = padded_2(grid_values, (("freq", 1), ("space", 0)), 3)
    first_y = lax.axis_index("freq") * band_rows - 3
    total_y = band_rows * lax.axis_size("freq")
    for sweep in range(3):
        padded = smooth_step(padded)
        global_x = first_x + sweep + 1 + jnp.arange(padded.shape[0], dtype=jnp.int32)
        global_y = first_y + sweep + 1 + jnp.arange(padded.shape[1], dtype=jnp.int32)
        valid_x = (global_x >= 0) & (global_x < total_x)
        valid_y = (global_y >= 0) & (global_y < total_y)
        padded = jnp.where(valid_x[:, None, None] & valid_y[None, :, None], padded, 0.0)
    return padded


def smooth(grid_values):
    return deep_smooth(grid_values)


def local(saved_modes, mode_gains):
    mode_count = saved_modes.shape[1]
    freq_total = saved_modes.shape[0] * lax.axis_size("freq")
    factor = -2.0 / (freq_total * mode_count)
    partial_terms = partial_sensitivity(saved_modes, mode_gains, factor)
    sensitivity = sum_at_owner(partial_terms, "freq", 1)
    return smooth(sensitivity)


def solution(mesh):
    in_specs = (P("freq", None, None, None, None, "space", None, None), P("freq", None))
    out_specs = P("space", "freq", None)
    return jax.shard_map(local, mesh=mesh, in_specs=in_specs, out_specs=out_specs, check_vma=False)
```

```python
import functools

import jax
import jax.numpy as jnp
from jax import lax
from jax.experimental import pallas as pl
from jax.experimental.pallas import tpu as pltpu
from jax.sharding import PartitionSpec as P

AXIAL = 0.35
CROSS = 0.06
PASSES = 3
MARGIN = 4
LATE_CHUNKS = 2
HELD_BACK = 4
MESH = pl.DeviceIdType.MESH


def diff_matrices(count):
    row = lax.broadcasted_iota(jnp.int32, (count, count), 0)
    col = lax.broadcasted_iota(jnp.int32, (count, count), 1)
    upper = (col == row + 1).astype(jnp.float32)
    lower = (col + 1 == row).astype(jnp.float32)
    along_rows = (upper - lower).astype(jnp.bfloat16)
    along_cols = (lower - upper).astype(jnp.bfloat16)
    return along_rows, along_cols


def strain_parts(field, x, diff_y, diff_z, low, high):
    center = [field[c, x] for c in range(3)]
    after = [field[c, x + 1].astype(jnp.float32) for c in range(3)]
    before = [field[c, x - 1].astype(jnp.float32) for c in range(3)]
    if high is not None:
        after = [value * high for value in after]
    if low is not None:
        before = [value * low for value in before]
    dx = [after[c] - before[c] for c in range(3)]
    dy = [jnp.dot(diff_y, center[c], preferred_element_type=jnp.float32) for c in range(3)]
    dz = [jnp.dot(center[c], diff_z, preferred_element_type=jnp.float32) for c in range(3)]
    return (dx[0], dy[1], dz[2], dx[1] + dy[0], dx[2] + dz[0], dy[2] + dz[1])


def pair_term(forward, adjoint, x, diff_y, diff_z, low=None, high=None):
    eu = strain_parts(forward, x, diff_y, diff_z, low, high)
    ev = strain_parts(adjoint, x, diff_y, diff_z, low, high)
    straight = eu[0] * ev[0] + eu[1] * ev[1] + eu[2] * ev[2]
    shear = eu[3] * ev[3] + eu[4] * ev[4] + eu[5] * ev[5]
    return straight + 0.5 * shear


def gradient_kernel(
    space,
    factor,
    modes,
    gains,
    out,
    buf,
    ymat,
    zmat,
    acc,
    rows_out,
    from_core,
    chip_sum,
    from_chip,
    from_side,
    grid0,
    grid1,
    grid2,
    load_sem,
    halo_sem,
    core_sem,
    chip_sem,
    side_sem,
):
    mode_count = modes.shape[1]
    planes = modes.shape[5]
    rows = modes.shape[6]
    cols = modes.shape[7]
    chunks = 2 * mode_count
    inner = planes - 2
    band = out.shape[1]
    block_rows = band + 2 * MARGIN
    me = lax.axis_index("space")
    freq = lax.axis_index("freq")
    core = lax.rem(freq, 2)
    chip = freq // 2
    other_core = freq + 1 - 2 * core
    other_chip = lax.rem(freq + 2, 4)
    above = lax.rem(me + 1, space)
    below = lax.rem(me + space - 1, space)

    def send(src, dst, sems, index, freq_to, space_to):
        return pltpu.make_async_remote_copy(
            src_ref=src,
            dst_ref=dst,
            send_sem=sems.at[(0, *index)],
            recv_sem=sems.at[(1, *index)],
            device_id={"freq": freq_to, "space": space_to},
            device_id_type=MESH,
        )

    def load(m):
        return pltpu.make_async_copy(
            modes.at[0, m], buf.at[m, :, :, :, pl.ds(1, planes)], load_sem.at[m]
        )

    def halo(c, side):
        m, part = c // 2, lax.rem(c, 2)
        plane, slot, target = (planes - 1, 0, above) if side == 0 else (0, planes + 1, below)
        return send(
            modes.at[0, m, :, part, :, plane],
            buf.at[m, :, part, :, slot],
            halo_sem,
            (side, c),
            freq,
            target,
        )

    def block(half, owner_core):
        start = pl.multiple_of((2 * half + owner_core) * band, 8)
        return pl.ds(start, block_rows)

    def to_core(late):
        first, count = (inner, 2) if late else (0, inner)
        return [
            send(
                rows_out.at[pl.ds(first, count), block(half, 1 - core)],
                from_core.at[half, pl.ds(first, count)],
                core_sem,
                (int(late), half),
                other_core,
                me,
            )
            for half in range(2)
        ]

    def to_chip(group):
        first, count = ((0, inner - HELD_BACK), (inner - HELD_BACK, HELD_BACK), (inner, 2))[group]
        return send(
            chip_sum.at[1 - chip, pl.ds(first, count)],
            from_chip.at[pl.ds(first, count)],
            chip_sem,
            (group,),
            other_chip,
            me,
        )

    def to_sides(late):
        spans = ((inner, 1, 2), (inner + 1, 1, 0)) if late else ((inner - 2, 2, 0), (0, 2, 1))
        copies = []
        for same in (1, 0):
            half, target_freq = (chip, freq) if same else (1 - chip, other_chip)
            for side, (first, count, slot) in enumerate(spans):
                copies.append(
                    send(
                        chip_sum.at[half, pl.ds(first, count)],
                        from_side.at[side, same, pl.ds(slot, count)],
                        side_sem,
                        (int(late), side, same),
                        target_freq,
                        above if side == 0 else below,
                    )
                )
        return copies

    def shift_rows(place):
        edge = jnp.zeros((MARGIN, cols), jnp.float32)
        rows_out[place] = jnp.concatenate([edge, acc[place], edge], axis=0)

    def add_cores(place):
        for half in range(2):
            chip_sum[half, place] = rows_out[place, block(half, core)] + from_core[half, place]

    load(0).start()
    barrier = pltpu.get_barrier_semaphore()
    for freq_to, space_to in (
        (freq, above),
        (freq, below),
        (other_core, me),
        (other_chip, me),
        (other_chip, above),
        (other_chip, below),
    ):
        pl.semaphore_signal(
            barrier, inc=1, device_id={"freq": freq_to, "space": space_to}, device_id_type=MESH
        )
    pl.semaphore_wait(barrier, 6)

    def start_halos(first, last):
        @pl.loop(first, last)
        def _(c):
            halo(c, 0).start()
            halo(c, 1).start()

    start_halos(0, chunks - LATE_CHUNKS)

    @pl.loop(1, mode_count)
    def _(m):
        load(m).start()

    diff_y, diff_z = diff_matrices(rows)
    ymat[...] = diff_y
    zmat[...] = diff_z
    acc[...] = jnp.zeros_like(acc)

    def term(m, part, x, low=None, high=None):
        return pair_term(
            buf.at[m, 0, part], buf.at[m, 1, part], x, ymat[...], zmat[...], low, high
        )

    @pl.loop(0, mode_count)
    def _(m):
        load(m).wait()
        weight = gains[0, m] * (0.25 * factor)

        @pl.loop(0, inner)
        def _(q):
            acc[q] += weight * (term(m, 0, q + 2) + term(m, 1, q + 2))

    @pl.loop(0, inner)
    def _(q):
        shift_rows(q)

    for copy in to_core(False):
        copy.start()
    for copy in to_core(False):
        copy.wait_recv()

    @pl.loop(0, inner)
    def _(q):
        add_cores(q)

    for copy in to_sides(False):
        copy.start()
    to_chip(0).start()
    start_halos(chunks - LATE_CHUNKS, chunks)
    to_chip(1).start()

    low = jnp.where(me > 0, 1.0, 0.0).astype(jnp.float32)
    high = jnp.where(me < space - 1, 1.0, 0.0).astype(jnp.float32)

    @pl.loop(0, chunks)
    def _(c):
        m, part = c // 2, lax.rem(c, 2)
        weight = gains[0, m] * (0.25 * factor)
        halo(c, 0).wait_recv()
        acc[inner + 1] += weight * term(m, part, 1, low=low)
        halo(c, 1).wait_recv()
        acc[inner] += weight * term(m, part, planes, high=high)

    shift_rows(inner)
    shift_rows(inner + 1)
    for copy in to_core(True):
        copy.start()
    for copy in to_core(True):
        copy.wait_recv()
    add_cores(inner)
    add_cores(inner + 1)
    to_chip(2).start()
    for copy in to_sides(True):
        copy.start()

    row = lax.broadcasted_iota(jnp.int32, (block_rows, cols), 0) + (freq * band - MARGIN)
    inside = ((row >= 0) & (row < rows)).astype(jnp.float32)
    col = lax.broadcasted_iota(jnp.int32, (block_rows, cols), 1)
    not_first = (col > 0).astype(jnp.float32)
    not_last = (col < cols - 1).astype(jnp.float32)

    def smoothed(source, i):
        center = source[i]
        axial = source[i + 1] + source[i - 1] - 2.0 * center
        cross = (
            pltpu.roll(center, 1, 0)
            + pltpu.roll(center, block_rows - 1, 0)
            + pltpu.roll(center, 1, 1) * not_first
            + pltpu.roll(center, cols - 1, 1) * not_last
            - 4.0 * center
        )
        return (center + AXIAL * axial + CROSS * cross) * inside

    def one_pass(step, first, last):
        source, target = ((grid0, grid1), (grid1, grid2), (grid2, None))[step]

        @pl.loop(first, last)
        def _(i):
            value = smoothed(source, i)
            if target is None:
                out[i - PASSES] = value[MARGIN : MARGIN + band]
            else:
                place = me * planes - PASSES + i
                kept = jnp.where((place >= 0) & (place < space * planes), 1.0, 0.0)
                target[i] = value * kept.astype(jnp.float32)

    to_chip(0).wait_recv()
    to_chip(1).wait_recv()

    @pl.loop(0, inner)
    def _(q):
        grid0[q + PASSES + 1] = chip_sum[chip, q] + from_chip[q]

    one_pass(0, PASSES + 2, PASSES + planes - 2)
    one_pass(1, PASSES + 3, PASSES + planes - 3)
    one_pass(2, PASSES + 4, PASSES + planes - 4)

    for copy in to_sides(False):
        copy.wait_recv()
    to_chip(2).wait_recv()
    for copy in to_sides(True):
        copy.wait_recv()
    grid0[PASSES + planes - 1] = chip_sum[chip, inner] + from_chip[inner]
    grid0[PASSES] = chip_sum[chip, inner + 1] + from_chip[inner + 1]
    for i in range(PASSES):
        grid0[i] = (from_side[0, 0, i] + from_side[0, 1, i]) * low
        grid0[PASSES + planes + i] = (from_side[1, 0, i] + from_side[1, 1, i]) * high
    for step in range(PASSES):
        one_pass(step, step + 1, PASSES + 2 + step)
        one_pass(step, PASSES + planes - 2 - step, 2 * PASSES + planes - 1 - step)

    @pl.loop(0, chunks)
    def _(c):
        halo(c, 0).wait_send()
        halo(c, 1).wait_send()

    for copy in (
        *to_core(False),
        *to_core(True),
        *(to_chip(group) for group in range(3)),
        *to_sides(False),
        *to_sides(True),
    ):
        copy.wait_send()


def local(saved_modes, mode_gains):
    freqs, mode_count, pair, parts, comps, planes, rows, cols = saved_modes.shape
    freq_total = freqs * lax.axis_size("freq")
    factor = -2.0 / (freq_total * mode_count)
    band = rows // freq_total
    block_rows = band + 2 * MARGIN
    padded_planes = planes + 2 * PASSES
    f32 = jnp.float32
    return pl.pallas_call(
        functools.partial(gradient_kernel, lax.axis_size("space"), factor),
        out_shape=jax.ShapeDtypeStruct((planes, band, cols), f32),
        in_specs=[
            pl.BlockSpec(memory_space=pl.ANY),
            pl.BlockSpec(memory_space=pltpu.SMEM),
        ],
        out_specs=pl.BlockSpec(memory_space=pltpu.VMEM),
        scratch_shapes=[
            pltpu.VMEM((mode_count, pair, parts, comps, planes + 2, rows, cols), jnp.bfloat16),
            pltpu.VMEM((rows, rows), jnp.bfloat16),
            pltpu.VMEM((cols, cols), jnp.bfloat16),
            pltpu.VMEM((planes, rows, cols), f32),
            pltpu.VMEM((planes, rows + 2 * MARGIN, cols), f32),
            pltpu.VMEM((2, planes, block_rows, cols), f32),
            pltpu.VMEM((2, planes, block_rows, cols), f32),
            pltpu.VMEM((planes, block_rows, cols), f32),
            pltpu.VMEM((2, 2, PASSES, block_rows, cols), f32),
            pltpu.VMEM((padded_planes, block_rows, cols), f32),
            pltpu.VMEM((padded_planes, block_rows, cols), f32),
            pltpu.VMEM((padded_planes, block_rows, cols), f32),
            pltpu.SemaphoreType.DMA((mode_count,)),
            pltpu.SemaphoreType.DMA((2, 2, 2 * mode_count)),
            pltpu.SemaphoreType.DMA((2, 2, 2)),
            pltpu.SemaphoreType.DMA((2, 3)),
            pltpu.SemaphoreType.DMA((2, 2, 2, 2)),
        ],
        compiler_params=pltpu.CompilerParams(
            collective_id=0, has_side_effects=True, vmem_limit_bytes=56 << 20
        ),
        name="gradient",
    )(saved_modes, mode_gains)


def solution(mesh):
    in_specs = (P("freq", None, None, None, None, "space", None, None), P("freq", None))
    out_specs = P("space", "freq", None)
    return jax.shard_map(local, mesh=mesh, in_specs=in_specs, out_specs=out_specs, check_vma=False)
```

```python
import functools

import jax
import jax.numpy as jnp
from jax import lax
from jax.experimental import pallas as pl
from jax.experimental.pallas import tpu as pltpu
from jax.sharding import PartitionSpec as P

AXIAL = 0.35
CROSS = 0.06
PASSES = 3
MARGIN = 4
LATE_CHUNKS = 2
HELD_BACK = 4
MESH = pl.DeviceIdType.MESH


def diff_matrices(count):
    row = lax.broadcasted_iota(jnp.int32, (count, count), 0)
    col = lax.broadcasted_iota(jnp.int32, (count, count), 1)
    upper = (col == row + 1).astype(jnp.float32)
    lower = (col + 1 == row).astype(jnp.float32)
    along_rows = (upper - lower).astype(jnp.bfloat16)
    along_cols = (lower - upper).astype(jnp.bfloat16)
    return along_rows, along_cols


def strain_parts(field, x, diff_y, diff_z):
    center = [field[c, x] for c in range(3)]
    after = [field[c, x + 1].astype(jnp.float32) for c in range(3)]
    before = [field[c, x - 1].astype(jnp.float32) for c in range(3)]
    dx = [after[c] - before[c] for c in range(3)]
    dy = [jnp.dot(diff_y, center[c], preferred_element_type=jnp.float32) for c in range(3)]
    dz = [jnp.dot(center[c], diff_z, preferred_element_type=jnp.float32) for c in range(3)]
    return (dx[0], dy[1], dz[2], dx[1] + dy[0], dx[2] + dz[0], dy[2] + dz[1])


def pair_term(forward, adjoint, x, diff_y, diff_z):
    eu = strain_parts(forward, x, diff_y, diff_z)
    ev = strain_parts(adjoint, x, diff_y, diff_z)
    straight = eu[0] * ev[0] + eu[1] * ev[1] + eu[2] * ev[2]
    shear = eu[3] * ev[3] + eu[4] * ev[4] + eu[5] * ev[5]
    return straight + 0.5 * shear


def gradient_kernel(
    space,
    factor,
    modes,
    gains,
    out,
    buf,
    ymat,
    zmat,
    acc,
    rows_out,
    from_core,
    chip_sum,
    from_chip,
    from_side,
    grid0,
    grid1,
    grid2,
    load_sem,
    halo_sem,
    core_sem,
    chip_sem,
    side_sem,
):
    mode_count = modes.shape[1]
    planes = modes.shape[5]
    rows = modes.shape[6]
    cols = modes.shape[7]
    chunks = 2 * mode_count
    inner = planes - 2
    band = out.shape[1]
    block_rows = band + 2 * MARGIN
    me = lax.axis_index("space")
    freq = lax.axis_index("freq")
    core = lax.rem(freq, 2)
    chip = freq // 2
    other_core = freq + 1 - 2 * core
    other_chip = lax.rem(freq + 2, 4)
    far = 1 - lax.rem(me, 2)
    near = 1 - far
    has_far = (me > 0) & (me < space - 1)

    def slab(side):
        return lax.rem(me + 1 - 2 * side + space, space)

    def send(src, dst, sems, index, freq_to, space_to):
        return pltpu.make_async_remote_copy(
            src_ref=src,
            dst_ref=dst,
            send_sem=sems.at[(0, *index)],
            recv_sem=sems.at[(1, *index)],
            device_id={"freq": freq_to, "space": space_to},
            device_id_type=MESH,
        )

    def load(m):
        return pltpu.make_async_copy(
            modes.at[0, m], buf.at[m, :, :, :, pl.ds(1, planes)], load_sem.at[m]
        )

    def halo(c, side):
        m, part = c // 2, lax.rem(c, 2)
        return send(
            modes.at[0, m, :, part, :, (planes - 1) * (1 - side)],
            buf.at[m, :, part, :, (planes + 1) * side],
            halo_sem,
            (side, c),
            freq,
            slab(side),
        )

    def block(half, owner_core):
        start = pl.multiple_of((2 * half + owner_core) * band, 8)
        return pl.ds(start, block_rows)

    def to_core(stage, first, count):
        return [
            send(
                rows_out.at[pl.ds(first, count), block(half, 1 - core)],
                from_core.at[half, pl.ds(first, count)],
                core_sem,
                (stage, half),
                other_core,
                me,
            )
            for half in range(2)
        ]

    def to_chip(group, first, count):
        return send(
            chip_sum.at[1 - chip, pl.ds(first, count)],
            from_chip.at[pl.ds(first, count)],
            chip_sem,
            (group,),
            other_chip,
            me,
        )

    def to_side(side, late, same):
        if late:
            first, count, slot = inner + side, 1, 2 - 2 * side
        else:
            first, count, slot = (inner - 2) * (1 - side), 2, side
        half, target_freq = (chip, freq) if same else (1 - chip, other_chip)
        return send(
            chip_sum.at[half, pl.ds(first, count)],
            from_side.at[side, same, pl.ds(slot, count)],
            side_sem,
            (side, int(late), same),
            target_freq,
            slab(side),
        )

    def bulk(group):
        return to_chip(group, *((0, inner - HELD_BACK), (inner - HELD_BACK, HELD_BACK))[group])

    def shift_rows(place):
        edge = jnp.zeros((MARGIN, cols), jnp.float32)
        rows_out[place] = jnp.concatenate([edge, acc[place], edge], axis=0)

    def add_cores(place):
        for half in range(2):
            chip_sum[half, place] = rows_out[place, block(half, core)] + from_core[half, place]

    load(0).start()
    barrier = pltpu.get_barrier_semaphore()

    def greet(freq_to, space_to):
        pl.semaphore_signal(
            barrier, inc=1, device_id={"freq": freq_to, "space": space_to}, device_id_type=MESH
        )

    @pl.when(has_far)
    def _():
        greet(freq, slab(far))
        greet(other_chip, slab(far))

    greet(freq, slab(near))
    greet(other_chip, slab(near))
    greet(other_chip, me)
    greet(other_core, me)
    pl.semaphore_wait(barrier, jnp.where(has_far, 6, 4))

    def start_halos(first, last):
        @pl.loop(first, last)
        def _(c):
            @pl.when(has_far)
            def _():
                halo(c, far).start()

            halo(c, near).start()

    start_halos(0, chunks - LATE_CHUNKS)

    @pl.loop(1, mode_count)
    def _(m):
        load(m).start()

    diff_y, diff_z = diff_matrices(rows)
    ymat[...] = diff_y
    zmat[...] = diff_z
    acc[...] = jnp.zeros_like(acc)

    @pl.when(jnp.logical_not(has_far))
    def _():
        @pl.loop(0, mode_count)
        def _(m):
            outer = buf.at[m, :, :, :, (planes + 1) * (1 - far)]
            outer[...] = jnp.zeros(outer.shape, outer.dtype)

        missing = from_side.at[1 - far]
        missing[...] = jnp.zeros(missing.shape, missing.dtype)

    def term(m, part, x):
        return pair_term(buf.at[m, 0, part], buf.at[m, 1, part], x, ymat[...], zmat[...])

    @pl.loop(0, mode_count)
    def _(m):
        load(m).wait()
        weight = gains[0, m] * (0.25 * factor)

        @pl.loop(0, inner)
        def _(q):
            acc[q] += weight * (term(m, 0, q + 2) + term(m, 1, q + 2))

    @pl.loop(0, inner)
    def _(q):
        shift_rows(q)

    early = to_core(0, 0, inner)
    for copy in early:
        copy.start()
    for copy in early:
        copy.wait_recv()

    @pl.loop(0, inner)
    def _(q):
        add_cores(q)

    @pl.when(has_far)
    def _():
        for same in (1, 0):
            to_side(far, False, same).start()

    for same in (1, 0):
        to_side(near, False, same).start()
    bulk(0).start()
    start_halos(chunks - LATE_CHUNKS, chunks)
    bulk(1).start()

    far_place = inner + far
    near_place = inner + near

    def late_core(stage):
        return to_core(stage, far_place if stage == 1 else near_place, 1)

    @pl.loop(0, 2 * chunks)
    def _(i):
        c, side = i // 2, lax.rem(i + far, 2)
        m, part = c // 2, lax.rem(c, 2)

        @pl.when((side == near) | has_far)
        def _():
            halo(c, 1 - side).wait_recv()

        weight = gains[0, m] * (0.25 * factor)
        acc[inner + side] += weight * term(m, part, planes - (planes - 1) * side)

        @pl.when(i == 2 * chunks - 2)
        def _():
            shift_rows(far_place)
            for copy in late_core(1):
                copy.start()

    shift_rows(near_place)
    for copy in late_core(2):
        copy.start()
    for copy in late_core(1):
        copy.wait_recv()
    add_cores(far_place)

    @pl.when(has_far)
    def _():
        for same in (1, 0):
            to_side(far, True, same).start()

    to_chip(2, far_place, 1).start()
    for copy in late_core(2):
        copy.wait_recv()
    add_cores(near_place)
    to_chip(3, near_place, 1).start()
    for same in (1, 0):
        to_side(near, True, same).start()

    row = lax.broadcasted_iota(jnp.int32, (block_rows, cols), 0) + (freq * band - MARGIN)
    inside = ((row >= 0) & (row < rows)).astype(jnp.float32)
    col = lax.broadcasted_iota(jnp.int32, (block_rows, cols), 1)
    not_first = (col > 0).astype(jnp.float32)
    not_last = (col < cols - 1).astype(jnp.float32)

    def smoothed(source, i):
        center = source[i]
        axial = source[i + 1] + source[i - 1] - 2.0 * center
        cross = (
            pltpu.roll(center, 1, 0)
            + pltpu.roll(center, block_rows - 1, 0)
            + pltpu.roll(center, 1, 1) * not_first
            + pltpu.roll(center, cols - 1, 1) * not_last
            - 4.0 * center
        )
        return (center + AXIAL * axial + CROSS * cross) * inside

    def one_pass(step, first, last):
        source, target = ((grid0, grid1), (grid1, grid2), (grid2, None))[step]

        @pl.loop(first, last)
        def _(i):
            value = smoothed(source, i)
            if target is None:
                out[i - PASSES] = value[MARGIN : MARGIN + band]
            else:
                place = me * planes - PASSES + i
                kept = jnp.where((place >= 0) & (place < space * planes), 1.0, 0.0)
                target[i] = value * kept.astype(jnp.float32)

    bulk(0).wait_recv()
    bulk(1).wait_recv()

    @pl.loop(0, inner)
    def _(q):
        grid0[q + PASSES + 1] = chip_sum[chip, q] + from_chip[q]

    one_pass(0, PASSES + 2, PASSES + planes - 2)
    one_pass(1, PASSES + 3, PASSES + planes - 3)
    one_pass(2, PASSES + 4, PASSES + planes - 4)

    def wait_sides(late):
        @pl.when(has_far)
        def _():
            for same in (1, 0):
                to_side(1 - far, late, same).wait_recv()

        for same in (1, 0):
            to_side(1 - near, late, same).wait_recv()

    wait_sides(False)
    to_chip(2, far_place, 1).wait_recv()
    to_chip(3, near_place, 1).wait_recv()
    wait_sides(True)
    grid0[PASSES + planes - 1] = chip_sum[chip, inner] + from_chip[inner]
    grid0[PASSES] = chip_sum[chip, inner + 1] + from_chip[inner + 1]
    for i in range(PASSES):
        grid0[i] = from_side[0, 0, i] + from_side[0, 1, i]
        grid0[PASSES + planes + i] = from_side[1, 0, i] + from_side[1, 1, i]
    for step in range(PASSES):
        one_pass(step, step + 1, PASSES + 2 + step)
        one_pass(step, PASSES + planes - 2 - step, 2 * PASSES + planes - 1 - step)

    @pl.loop(0, chunks)
    def _(c):
        @pl.when(has_far)
        def _():
            halo(c, far).wait_send()

        halo(c, near).wait_send()

    @pl.when(has_far)
    def _():
        for late in (False, True):
            for same in (1, 0):
                to_side(far, late, same).wait_send()

    for copy in (
        *early,
        *late_core(1),
        *late_core(2),
        bulk(0),
        bulk(1),
        to_chip(2, far_place, 1),
        to_chip(3, near_place, 1),
        *(to_side(near, late, same) for late in (False, True) for same in (1, 0)),
    ):
        copy.wait_send()


def local(saved_modes, mode_gains):
    freqs, mode_count, pair, parts, comps, planes, rows, cols = saved_modes.shape
    freq_total = freqs * lax.axis_size("freq")
    factor = -2.0 / (freq_total * mode_count)
    band = rows // freq_total
    block_rows = band + 2 * MARGIN
    padded_planes = planes + 2 * PASSES
    f32 = jnp.float32
    return pl.pallas_call(
        functools.partial(gradient_kernel, lax.axis_size("space"), factor),
        out_shape=jax.ShapeDtypeStruct((planes, band, cols), f32),
        in_specs=[
            pl.BlockSpec(memory_space=pl.ANY),
            pl.BlockSpec(memory_space=pltpu.SMEM),
        ],
        out_specs=pl.BlockSpec(memory_space=pltpu.VMEM),
        scratch_shapes=[
            pltpu.VMEM((mode_count, pair, parts, comps, planes + 2, rows, cols), jnp.bfloat16),
            pltpu.VMEM((rows, rows), jnp.bfloat16),
            pltpu.VMEM((cols, cols), jnp.bfloat16),
            pltpu.VMEM((planes, rows, cols), f32),
            pltpu.VMEM((planes, rows + 2 * MARGIN, cols), f32),
            pltpu.VMEM((2, planes, block_rows, cols), f32),
            pltpu.VMEM((2, planes, block_rows, cols), f32),
            pltpu.VMEM((planes, block_rows, cols), f32),
            pltpu.VMEM((2, 2, PASSES, block_rows, cols), f32),
            pltpu.VMEM((padded_planes, block_rows, cols), f32),
            pltpu.VMEM((padded_planes, block_rows, cols), f32),
            pltpu.VMEM((padded_planes, block_rows, cols), f32),
            pltpu.SemaphoreType.DMA((mode_count,)),
            pltpu.SemaphoreType.DMA((2, 2, 2 * mode_count)),
            pltpu.SemaphoreType.DMA((2, 3, 2)),
            pltpu.SemaphoreType.DMA((2, 4)),
            pltpu.SemaphoreType.DMA((2, 2, 2, 2)),
        ],
        compiler_params=pltpu.CompilerParams(
            collective_id=0, has_side_effects=True, vmem_limit_bytes=40 << 20
        ),
        name="gradient",
    )(saved_modes, mode_gains)


def solution(mesh):
    in_specs = (P("freq", None, None, None, None, "space", None, None), P("freq", None))
    out_specs = P("space", "freq", None)
    return jax.shard_map(local, mesh=mesh, in_specs=in_specs, out_specs=out_specs, check_vma=False)
```

```python
import functools

import jax
import jax.numpy as jnp
from jax import lax
from jax.experimental import pallas as pl
from jax.experimental.pallas import tpu as pltpu
from jax.sharding import PartitionSpec as P

AXIAL = 0.35
CROSS = 0.06
PASSES = 3
MARGIN = 4
LATE_CHUNKS = 2
HELD_BACK = 6
MESH = pl.DeviceIdType.MESH


def diff_matrices(count):
    row = lax.broadcasted_iota(jnp.int32, (count, count), 0)
    col = lax.broadcasted_iota(jnp.int32, (count, count), 1)
    upper = (col == row + 1).astype(jnp.float32)
    lower = (col + 1 == row).astype(jnp.float32)
    along_rows = (upper - lower).astype(jnp.bfloat16)
    along_cols = (lower - upper).astype(jnp.bfloat16)
    return along_rows, along_cols


def strain_parts(field, x, diff_y, diff_z):
    center = [field[c, x] for c in range(3)]
    after = [field[c, x + 1].astype(jnp.float32) for c in range(3)]
    before = [field[c, x - 1].astype(jnp.float32) for c in range(3)]
    dx = [after[c] - before[c] for c in range(3)]
    dy = [jnp.dot(diff_y, center[c], preferred_element_type=jnp.float32) for c in range(3)]
    dz = [jnp.dot(center[c], diff_z, preferred_element_type=jnp.float32) for c in range(3)]
    return (dx[0], dy[1], dz[2], dx[1] + dy[0], dx[2] + dz[0], dy[2] + dz[1])


def pair_term(forward, adjoint, x, diff_y, diff_z):
    eu = strain_parts(forward, x, diff_y, diff_z)
    ev = strain_parts(adjoint, x, diff_y, diff_z)
    straight = eu[0] * ev[0] + eu[1] * ev[1] + eu[2] * ev[2]
    shear = eu[3] * ev[3] + eu[4] * ev[4] + eu[5] * ev[5]
    return straight + 0.5 * shear


def gradient_kernel(
    space,
    factor,
    modes,
    gains,
    out,
    buf,
    ymat,
    zmat,
    acc,
    rows_out,
    from_core,
    chip_sum,
    smooth_sum,
    from_chip,
    late_chip,
    from_side,
    late_side,
    grid0,
    grid1,
    grid2,
    late0,
    late1,
    late2,
    load_sem,
    halo_sem,
    core_sem,
    chip_sem,
    side_sem,
):
    mode_count = modes.shape[1]
    planes = modes.shape[5]
    rows = modes.shape[6]
    cols = modes.shape[7]
    chunks = 2 * mode_count
    inner = planes - 2
    band = out.shape[1]
    block_rows = band + 2 * MARGIN
    me = lax.axis_index("space")
    freq = lax.axis_index("freq")
    core = lax.rem(freq, 2)
    chip = freq // 2
    other_core = freq + 1 - 2 * core
    other_chip = lax.rem(freq + 2, 4)
    far = 1 - lax.rem(me, 2)
    near = 1 - far
    has_far = (me > 0) & (me < space - 1)

    def slab(side):
        return lax.rem(me + 1 - 2 * side + space, space)

    def send(src, dst, sems, index, freq_to, space_to):
        return pltpu.make_async_remote_copy(
            src_ref=src,
            dst_ref=dst,
            send_sem=sems.at[(0, *index)],
            recv_sem=sems.at[(1, *index)],
            device_id={"freq": freq_to, "space": space_to},
            device_id_type=MESH,
        )

    def load(m):
        return pltpu.make_async_copy(
            modes.at[0, m], buf.at[m, :, :, :, pl.ds(1, planes)], load_sem.at[m]
        )

    def halo(c, side):
        m, part = c // 2, lax.rem(c, 2)
        return send(
            modes.at[0, m, :, part, :, (planes - 1) * (1 - side)],
            buf.at[m, :, part, :, (planes + 1) * side],
            halo_sem,
            (side, c),
            freq,
            slab(side),
        )

    def block(half, owner_core):
        start = pl.multiple_of((2 * half + owner_core) * band, 8)
        return pl.ds(start, block_rows)

    def to_core(stage, first, count):
        return [
            send(
                rows_out.at[pl.ds(first, count), block(half, 1 - core)],
                from_core.at[half, pl.ds(first, count)],
                core_sem,
                (stage, half),
                other_core,
                me,
            )
            for half in range(2)
        ]

    def bulk(group):
        split = planes - HELD_BACK
        first, count = ((0, split), (split, HELD_BACK))[group]
        return send(
            smooth_sum.at[pl.ds(first, count)],
            from_chip.at[pl.ds(first, count)],
            chip_sem,
            (group,),
            other_chip,
            me,
        )

    def late_to_chip(side):
        return send(
            chip_sum.at[1 - chip, inner + side],
            late_chip.at[side],
            chip_sem,
            (2 + side,),
            other_chip,
            me,
        )

    def early_to_side(side, half):
        return send(
            chip_sum.at[half, pl.ds((inner - 2) * (1 - side), 2)],
            from_side.at[side, half],
            side_sem,
            (side, half),
            other_chip,
            slab(side),
        )

    def late_to_side(side, same):
        half, target_freq = (chip, freq) if same else (1 - chip, other_chip)
        return send(
            chip_sum.at[half, inner + side],
            late_side.at[side, same],
            side_sem,
            (side, 2 + same),
            target_freq,
            slab(side),
        )

    def shift_rows(place):
        edge = jnp.zeros((MARGIN, cols), jnp.float32)
        rows_out[place] = jnp.concatenate([edge, acc[place], edge], axis=0)

    def add_cores(place):
        for half in range(2):
            chip_sum[half, place] = rows_out[place, block(half, core)] + from_core[half, place]

    load(0).start()
    barrier = pltpu.get_barrier_semaphore()

    def greet(freq_to, space_to):
        pl.semaphore_signal(
            barrier, inc=1, device_id={"freq": freq_to, "space": space_to}, device_id_type=MESH
        )

    @pl.when(has_far)
    def _():
        greet(freq, slab(far))
        greet(other_chip, slab(far))

    greet(freq, slab(near))
    greet(other_chip, slab(near))
    greet(other_chip, me)
    greet(other_core, me)
    pl.semaphore_wait(barrier, jnp.where(has_far, 6, 4))

    def start_halos(first, last):
        @pl.loop(first, last)
        def _(c):
            @pl.when(has_far)
            def _():
                halo(c, far).start()

            halo(c, near).start()

    start_halos(0, chunks - LATE_CHUNKS)

    @pl.loop(1, mode_count)
    def _(m):
        load(m).start()

    diff_y, diff_z = diff_matrices(rows)
    ymat[...] = diff_y
    zmat[...] = diff_z
    acc[...] = jnp.zeros_like(acc)

    @pl.when(jnp.logical_not(has_far))
    def _():
        @pl.loop(0, mode_count)
        def _(m):
            outer = buf.at[m, :, :, :, (planes + 1) * (1 - far)]
            outer[...] = jnp.zeros(outer.shape, outer.dtype)

        for landing in (from_side, late_side):
            missing = landing.at[1 - far]
            missing[...] = jnp.zeros(missing.shape, missing.dtype)

    def term(m, part, x):
        return pair_term(buf.at[m, 0, part], buf.at[m, 1, part], x, ymat[...], zmat[...])

    @pl.loop(0, mode_count)
    def _(m):
        load(m).wait()
        weight = gains[0, m] * (0.25 * factor)

        @pl.loop(0, inner)
        def _(q):
            acc[q] += weight * (term(m, 0, q + 2) + term(m, 1, q + 2))

    @pl.loop(0, inner)
    def _(q):
        shift_rows(q)

    early = to_core(0, 0, inner)
    for copy in early:
        copy.start()
    for copy in early:
        copy.wait_recv()

    @pl.loop(0, inner)
    def _(q):
        add_cores(q)

    @pl.when(has_far)
    def _():
        for half in range(2):
            early_to_side(far, half).start()

    for half in range(2):
        early_to_side(near, half).start()

    row = lax.broadcasted_iota(jnp.int32, (block_rows, cols), 0) - MARGIN
    col = lax.broadcasted_iota(jnp.int32, (block_rows, cols), 1)
    not_first = (col > 0).astype(jnp.float32)
    not_last = (col < cols - 1).astype(jnp.float32)

    def smoothed(source, i):
        center = source[i]
        axial = source[i + 1] + source[i - 1] - 2.0 * center
        cross = (
            pltpu.roll(center, 1, 0)
            + pltpu.roll(center, block_rows - 1, 0)
            + pltpu.roll(center, 1, 1) * not_first
            + pltpu.roll(center, cols - 1, 1) * not_last
            - 4.0 * center
        )
        return center + AXIAL * axial + CROSS * cross

    def one_pass(source, target, half, first, count, width):
        at_row = row + (2 * half + core) * band
        inside = ((at_row >= 0) & (at_row < rows)).astype(jnp.float32)

        @pl.loop(0, count // width)
        def _(k):
            for j in range(width):
                i = first + k * width + j
                place = me * planes - PASSES + i
                kept = jnp.where((place >= 0) & (place < space * planes), 1.0, 0.0)
                target[i] = smoothed(source, i) * (inside * kept.astype(jnp.float32))

    def last_pass(source, first, count, width, store):
        @pl.loop(0, count // width)
        def _(k):
            for j in range(width):
                i = first + k * width + j
                store(i - PASSES, smoothed(source, i)[MARGIN : MARGIN + band])

    def smooth_early(half, store):
        @pl.loop(0, inner)
        def _(q):
            grid0[q + PASSES + 1] = chip_sum[half, q]

        for i in range(2):
            grid0[i] = from_side[0, half, i]
            grid0[PASSES + planes + 1 + i] = from_side[1, half, i]
        one_pass(grid0, grid1, half, 1, planes + 4, 2)
        one_pass(grid1, grid2, half, 2, planes + 2, 2)
        last_pass(grid2, 3, planes, 2, store)

    def keep(p, value):
        out[p] = value

    def pass_on(p, value):
        smooth_sum[p] = value

    for edge in (grid0, late0, late1, late2):
        edge[...] = jnp.zeros_like(edge)

    @pl.when(has_far)
    def _():
        for half in range(2):
            early_to_side(1 - far, half).wait_recv()

    for half in range(2):
        early_to_side(1 - near, half).wait_recv()
    smooth_early(1 - chip, pass_on)
    bulk(0).start()
    start_halos(chunks - LATE_CHUNKS, chunks)
    bulk(1).start()
    smooth_early(chip, keep)

    far_place = inner + far
    near_place = inner + near

    def late_core(stage):
        return to_core(stage, far_place if stage == 1 else near_place, 1)

    @pl.loop(0, 2 * chunks)
    def _(i):
        c, side = i // 2, lax.rem(i + far, 2)
        m, part = c // 2, lax.rem(c, 2)

        @pl.when((side == near) | has_far)
        def _():
            halo(c, 1 - side).wait_recv()

        weight = gains[0, m] * (0.25 * factor)
        acc[inner + side] += weight * term(m, part, planes - (planes - 1) * side)

        @pl.when(i == 2 * chunks - 2)
        def _():
            shift_rows(far_place)
            for copy in late_core(1):
                copy.start()

    shift_rows(near_place)
    for copy in late_core(2):
        copy.start()
    for copy in late_core(1):
        copy.wait_recv()
    add_cores(far_place)

    @pl.when(has_far)
    def _():
        for same in (1, 0):
            late_to_side(far, same).start()

    late_to_chip(far).start()
    for copy in late_core(2):
        copy.wait_recv()
    add_cores(near_place)
    late_to_chip(near).start()
    for same in (1, 0):
        late_to_side(near, same).start()

    bulk(0).wait_recv()
    bulk(1).wait_recv()

    @pl.loop(0, planes)
    def _(p):
        out[p] += from_chip[p]

    def add_late(p, value):
        out[p] += value

    def smooth_late(side):
        late0[PASSES + (planes - 1) * (1 - side)] = chip_sum[chip, inner + side] + late_chip[side]
        late0[PASSES - 1 + (planes + 1) * (1 - side)] = (
            late_side[1 - side, 0] + late_side[1 - side, 1]
        )
        start = [(planes + 1 - step) * (1 - side) + (1 + step) * side for step in range(PASSES)]
        one_pass(late0, late1, chip, start[0], 4, 4)
        one_pass(late1, late2, chip, start[1], 4, 4)
        last_pass(late2, start[2], 4, 4, add_late)

    late_to_chip(far).wait_recv()

    @pl.when(has_far)
    def _():
        for same in (1, 0):
            late_to_side(1 - far, same).wait_recv()

    smooth_late(far)
    late_to_chip(near).wait_recv()
    for same in (1, 0):
        late_to_side(1 - near, same).wait_recv()
    smooth_late(near)

    @pl.loop(0, chunks)
    def _(c):
        @pl.when(has_far)
        def _():
            halo(c, far).wait_send()

        halo(c, near).wait_send()

    def to_side(side):
        return (
            *(early_to_side(side, half) for half in range(2)),
            *(late_to_side(side, same) for same in (1, 0)),
        )

    @pl.when(has_far)
    def _():
        for copy in to_side(far):
            copy.wait_send()

    for copy in (
        *early,
        *late_core(1),
        *late_core(2),
        bulk(0),
        bulk(1),
        late_to_chip(far),
        late_to_chip(near),
        *to_side(near),
    ):
        copy.wait_send()


def local(saved_modes, mode_gains):
    freqs, mode_count, pair, parts, comps, planes, rows, cols = saved_modes.shape
    freq_total = freqs * lax.axis_size("freq")
    factor = -2.0 / (freq_total * mode_count)
    band = rows // freq_total
    block_rows = band + 2 * MARGIN
    padded_planes = planes + 2 * PASSES
    f32 = jnp.float32
    return pl.pallas_call(
        functools.partial(gradient_kernel, lax.axis_size("space"), factor),
        out_shape=jax.ShapeDtypeStruct((planes, band, cols), f32),
        in_specs=[
            pl.BlockSpec(memory_space=pl.ANY),
            pl.BlockSpec(memory_space=pltpu.SMEM),
        ],
        out_specs=pl.BlockSpec(memory_space=pltpu.VMEM),
        scratch_shapes=[
            pltpu.VMEM((mode_count, pair, parts, comps, planes + 2, rows, cols), jnp.bfloat16),
            pltpu.VMEM((rows, rows), jnp.bfloat16),
            pltpu.VMEM((cols, cols), jnp.bfloat16),
            pltpu.VMEM((planes, rows, cols), f32),
            pltpu.VMEM((planes, rows + 2 * MARGIN, cols), f32),
            pltpu.VMEM((2, planes, block_rows, cols), f32),
            pltpu.VMEM((2, planes, block_rows, cols), f32),
            pltpu.VMEM((planes, band, cols), f32),
            pltpu.VMEM((planes, band, cols), f32),
            pltpu.VMEM((2, block_rows, cols), f32),
            pltpu.VMEM((2, 2, 2, block_rows, cols), f32),
            pltpu.VMEM((2, 2, block_rows, cols), f32),
            pltpu.VMEM((padded_planes, block_rows, cols), f32),
            pltpu.VMEM((padded_planes, block_rows, cols), f32),
            pltpu.VMEM((padded_planes, block_rows, cols), f32),
            pltpu.VMEM((padded_planes, block_rows, cols), f32),
            pltpu.VMEM((padded_planes, block_rows, cols), f32),
            pltpu.VMEM((padded_planes, block_rows, cols), f32),
            pltpu.SemaphoreType.DMA((mode_count,)),
            pltpu.SemaphoreType.DMA((2, 2, 2 * mode_count)),
            pltpu.SemaphoreType.DMA((2, 3, 2)),
            pltpu.SemaphoreType.DMA((2, 4)),
            pltpu.SemaphoreType.DMA((2, 2, 4)),
        ],
        compiler_params=pltpu.CompilerParams(
            collective_id=0, has_side_effects=True, vmem_limit_bytes=40 << 20
        ),
        name="gradient",
    )(saved_modes, mode_gains)


def solution(mesh):
    in_specs = (P("freq", None, None, None, None, "space", None, None), P("freq", None))
    out_specs = P("space", "freq", None)
    return jax.shard_map(local, mesh=mesh, in_specs=in_specs, out_specs=out_specs, check_vma=False)
```

```python
import functools

import jax
import jax.numpy as jnp
from jax import lax
from jax.experimental import pallas as pl
from jax.experimental.pallas import tpu as pltpu
from jax.sharding import PartitionSpec as P

AXIAL = 0.35
CROSS = 0.06
PASSES = 3
MARGIN = 4
LATE_CHUNKS = 2
HELD_BACK = 10
MESH = pl.DeviceIdType.MESH


def diff_matrices(count):
    row = lax.broadcasted_iota(jnp.int32, (count, count), 0)
    col = lax.broadcasted_iota(jnp.int32, (count, count), 1)
    upper = (col == row + 1).astype(jnp.float32)
    lower = (col + 1 == row).astype(jnp.float32)
    along_rows = (upper - lower).astype(jnp.bfloat16)
    along_cols = (lower - upper).astype(jnp.bfloat16)
    return along_rows, along_cols


def strain_parts(field, x, diff_y, diff_z):
    center = [field[c, x] for c in range(3)]
    after = [field[c, x + 1].astype(jnp.float32) for c in range(3)]
    before = [field[c, x - 1].astype(jnp.float32) for c in range(3)]
    dx = [after[c] - before[c] for c in range(3)]
    dy = [jnp.dot(diff_y, center[c], preferred_element_type=jnp.float32) for c in range(3)]
    dz = [jnp.dot(center[c], diff_z, preferred_element_type=jnp.float32) for c in range(3)]
    return (dx[0], dy[1], dz[2], dx[1] + dy[0], dx[2] + dz[0], dy[2] + dz[1])


def pair_term(forward, adjoint, x, diff_y, diff_z):
    eu = strain_parts(forward, x, diff_y, diff_z)
    ev = strain_parts(adjoint, x, diff_y, diff_z)
    straight = eu[0] * ev[0] + eu[1] * ev[1] + eu[2] * ev[2]
    shear = eu[3] * ev[3] + eu[4] * ev[4] + eu[5] * ev[5]
    return straight + 0.5 * shear


def gradient_kernel(
    space,
    factor,
    modes,
    gains,
    out,
    buf,
    ymat,
    zmat,
    acc,
    rows_out,
    from_core,
    chip_sum,
    smooth_sum,
    from_chip,
    late_chip,
    from_side,
    late_side,
    grid0,
    grid1,
    grid2,
    late0,
    late1,
    late2,
    load_sem,
    halo_sem,
    core_sem,
    chip_sem,
    side_sem,
    core_in,
    chip_in,
):
    mode_count = modes.shape[1]
    planes = modes.shape[5]
    rows = modes.shape[6]
    cols = modes.shape[7]
    chunks = 2 * mode_count
    inner = planes - 2
    band = out.shape[1]
    block_rows = band + 2 * MARGIN
    me = lax.axis_index("space")
    freq = lax.axis_index("freq")
    core = lax.rem(freq, 2)
    chip = freq // 2
    other_core = freq + 1 - 2 * core
    other_chip = lax.rem(freq + 2, 4)
    far = 1 - lax.rem(me, 2)
    near = 1 - far
    has_far = (me > 0) & (me < space - 1)

    def slab(side):
        return lax.rem(me + 1 - 2 * side + space, space)

    def send(src, dst, sems, index, freq_to, space_to):
        return pltpu.make_async_remote_copy(
            src_ref=src,
            dst_ref=dst,
            send_sem=sems.at[(0, *index)],
            recv_sem=sems.at[(1, *index)],
            device_id={"freq": freq_to, "space": space_to},
            device_id_type=MESH,
        )

    def load(m):
        return pltpu.make_async_copy(
            modes.at[0, m], buf.at[m, :, :, :, pl.ds(1, planes)], load_sem.at[m]
        )

    def halo(c, side):
        m, part = c // 2, lax.rem(c, 2)
        return send(
            modes.at[0, m, :, part, :, (planes - 1) * (1 - side)],
            buf.at[m, :, part, :, (planes + 1) * side],
            halo_sem,
            (side, c),
            freq,
            slab(side),
        )

    def block(half, owner_core):
        start = pl.multiple_of((2 * half + owner_core) * band, 8)
        return pl.ds(start, block_rows)

    def to_core(stage, first, count):
        return [
            send(
                rows_out.at[pl.ds(first, count), block(half, 1 - core)],
                from_core.at[half, pl.ds(first, count)],
                core_sem,
                (stage, half),
                other_core,
                me,
            )
            for half in range(2)
        ]

    def bulk(group):
        split = planes - HELD_BACK
        first, count = ((0, split), (split, HELD_BACK))[group]
        return send(
            smooth_sum.at[pl.ds(first, count)],
            from_chip.at[pl.ds(first, count)],
            chip_sem,
            (group,),
            other_chip,
            me,
        )

    def late_to_chip(side):
        return send(
            chip_sum.at[1 - chip, inner + side],
            late_chip.at[side],
            chip_sem,
            (2 + side,),
            other_chip,
            me,
        )

    def early_to_side(side, half):
        return send(
            chip_sum.at[half, pl.ds((inner - 2) * (1 - side), 2)],
            from_side.at[side, half],
            side_sem,
            (side, half),
            other_chip,
            slab(side),
        )

    def late_to_side(side, same):
        half, target_freq = (chip, freq) if same else (1 - chip, other_chip)
        return send(
            chip_sum.at[half, inner + side],
            late_side.at[side, same],
            side_sem,
            (side, 2 + same),
            target_freq,
            slab(side),
        )

    def shift_rows(place):
        edge = jnp.zeros((MARGIN, cols), jnp.float32)
        rows_out[place] = jnp.concatenate([edge, acc[place], edge], axis=0)

    def add_cores(place):
        for half in range(2):
            chip_sum[half, place] = rows_out[place, block(half, core)] + from_core[half, place]

    load(0).start()
    barrier = pltpu.get_barrier_semaphore()

    def greet(freq_to, space_to):
        pl.semaphore_signal(
            barrier, inc=1, device_id={"freq": freq_to, "space": space_to}, device_id_type=MESH
        )

    @pl.when(has_far)
    def _():
        greet(freq, slab(far))

    greet(freq, slab(near))

    @pl.when(core == 0)
    def _():
        greet(other_core, me)

    @pl.when(chip == 0)
    def _():
        greet(other_chip, me)

    pl.semaphore_wait(barrier, jnp.where(has_far, 2, 1) + core + chip)

    def start_halos(first, last):
        @pl.loop(first, last)
        def _(c):
            @pl.when(has_far)
            def _():
                halo(c, far).start()

            halo(c, near).start()

    start_halos(0, chunks - LATE_CHUNKS)

    def answer(sem, freq_to):
        pl.semaphore_signal(
            sem, inc=1, device_id={"freq": freq_to, "space": me}, device_id_type=MESH
        )

    @pl.when(core == 1)
    def _():
        answer(core_in, other_core)

    @pl.when(chip == 1)
    def _():
        answer(chip_in, other_chip)

    @pl.loop(1, mode_count)
    def _(m):
        load(m).start()

    diff_y, diff_z = diff_matrices(rows)
    ymat[...] = diff_y
    zmat[...] = diff_z
    acc[...] = jnp.zeros_like(acc)

    @pl.when(jnp.logical_not(has_far))
    def _():
        @pl.loop(0, mode_count)
        def _(m):
            outer = buf.at[m, :, :, :, (planes + 1) * (1 - far)]
            outer[...] = jnp.zeros(outer.shape, outer.dtype)

        for landing in (from_side, late_side):
            missing = landing.at[1 - far]
            missing[...] = jnp.zeros(missing.shape, missing.dtype)

    def term(m, part, x):
        return pair_term(buf.at[m, 0, part], buf.at[m, 1, part], x, ymat[...], zmat[...])

    @pl.loop(0, mode_count)
    def _(m):
        load(m).wait()
        weight = gains[0, m] * (0.25 * factor)

        @pl.loop(0, inner)
        def _(q):
            acc[q] += weight * (term(m, 0, q + 2) + term(m, 1, q + 2))

    @pl.loop(0, inner)
    def _(q):
        shift_rows(q)

    @pl.when(core == 0)
    def _():
        pl.semaphore_wait(core_in, 1)

    @pl.when(chip == 0)
    def _():
        pl.semaphore_wait(chip_in, 1)
        answer(chip_in, other_chip)

    early = to_core(0, 0, inner)
    for copy in early:
        copy.start()
    for copy in early:
        copy.wait_recv()

    @pl.loop(0, inner)
    def _(q):
        add_cores(q)

    @pl.when(chip == 1)
    def _():
        pl.semaphore_wait(chip_in, 1)

    @pl.when(has_far)
    def _():
        for half in range(2):
            early_to_side(far, half).start()

    for half in range(2):
        early_to_side(near, half).start()

    row = lax.broadcasted_iota(jnp.int32, (block_rows, cols), 0) - MARGIN
    col = lax.broadcasted_iota(jnp.int32, (block_rows, cols), 1)
    not_first = (col > 0).astype(jnp.float32)
    not_last = (col < cols - 1).astype(jnp.float32)

    def smoothed(source, i):
        center = source[i]
        axial = source[i + 1] + source[i - 1] - 2.0 * center
        cross = (
            pltpu.roll(center, 1, 0)
            + pltpu.roll(center, block_rows - 1, 0)
            + pltpu.roll(center, 1, 1) * not_first
            + pltpu.roll(center, cols - 1, 1) * not_last
            - 4.0 * center
        )
        return center + AXIAL * axial + CROSS * cross

    def one_pass(source, target, half, first, count, width):
        at_row = row + (2 * half + core) * band
        inside = ((at_row >= 0) & (at_row < rows)).astype(jnp.float32)

        @pl.loop(0, count // width)
        def _(k):
            for j in range(width):
                i = first + k * width + j
                place = me * planes - PASSES + i
                kept = jnp.where((place >= 0) & (place < space * planes), 1.0, 0.0)
                target[i] = smoothed(source, i) * (inside * kept.astype(jnp.float32))

    def last_pass(source, first, count, width, store):
        @pl.loop(0, count // width)
        def _(k):
            for j in range(width):
                i = first + k * width + j
                store(i - PASSES, smoothed(source, i)[MARGIN : MARGIN + band])

    def smooth_early(half, store):
        @pl.loop(0, inner)
        def _(q):
            grid0[q + PASSES + 1] = chip_sum[half, q]

        for i in range(2):
            grid0[i] = from_side[0, half, i]
            grid0[PASSES + planes + 1 + i] = from_side[1, half, i]
        one_pass(grid0, grid1, half, 1, planes + 4, 2)
        one_pass(grid1, grid2, half, 2, planes + 2, 2)
        last_pass(grid2, 3, planes, 2, store)

    def keep(p, value):
        out[p] = value

    def pass_on(p, value):
        smooth_sum[p] = value

    for edge in (grid0, late0, late1, late2):
        edge[...] = jnp.zeros_like(edge)

    @pl.when(has_far)
    def _():
        for half in range(2):
            early_to_side(1 - far, half).wait_recv()

    for half in range(2):
        early_to_side(1 - near, half).wait_recv()
    smooth_early(1 - chip, pass_on)
    bulk(0).start()
    start_halos(chunks - LATE_CHUNKS, chunks)
    bulk(1).start()
    smooth_early(chip, keep)

    far_place = inner + far
    near_place = inner + near

    def late_core(stage):
        return to_core(stage, far_place if stage == 1 else near_place, 1)

    @pl.loop(0, 2 * chunks)
    def _(i):
        c, side = i // 2, lax.rem(i + far, 2)
        m, part = c // 2, lax.rem(c, 2)

        @pl.when((side == near) | has_far)
        def _():
            halo(c, 1 - side).wait_recv()

        weight = gains[0, m] * (0.25 * factor)
        acc[inner + side] += weight * term(m, part, planes - (planes - 1) * side)

        @pl.when(i == 2 * chunks - 2)
        def _():
            shift_rows(far_place)
            for copy in late_core(1):
                copy.start()

    shift_rows(near_place)
    for copy in late_core(2):
        copy.start()
    for copy in late_core(1):
        copy.wait_recv()
    add_cores(far_place)

    @pl.when(has_far)
    def _():
        for same in (1, 0):
            late_to_side(far, same).start()

    late_to_chip(far).start()
    for copy in late_core(2):
        copy.wait_recv()
    add_cores(near_place)
    late_to_chip(near).start()
    for same in (1, 0):
        late_to_side(near, same).start()

    bulk(0).wait_recv()
    bulk(1).wait_recv()

    @pl.loop(0, planes)
    def _(p):
        out[p] += from_chip[p]

    def add_late(p, value):
        out[p] += value

    def smooth_late(side):
        late0[PASSES + (planes - 1) * (1 - side)] = chip_sum[chip, inner + side] + late_chip[side]
        late0[PASSES - 1 + (planes + 1) * (1 - side)] = (
            late_side[1 - side, 0] + late_side[1 - side, 1]
        )
        start = [(planes + 1 - step) * (1 - side) + (1 + step) * side for step in range(PASSES)]
        one_pass(late0, late1, chip, start[0], 4, 4)
        one_pass(late1, late2, chip, start[1], 4, 4)
        last_pass(late2, start[2], 4, 4, add_late)

    late_to_chip(far).wait_recv()

    @pl.when(has_far)
    def _():
        for same in (1, 0):
            late_to_side(1 - far, same).wait_recv()

    smooth_late(far)
    late_to_chip(near).wait_recv()
    for same in (1, 0):
        late_to_side(1 - near, same).wait_recv()
    smooth_late(near)

    @pl.loop(0, chunks)
    def _(c):
        @pl.when(has_far)
        def _():
            halo(c, far).wait_send()

        halo(c, near).wait_send()

    def to_side(side):
        return (
            *(early_to_side(side, half) for half in range(2)),
            *(late_to_side(side, same) for same in (1, 0)),
        )

    @pl.when(has_far)
    def _():
        for copy in to_side(far):
            copy.wait_send()

    for copy in (
        *early,
        *late_core(1),
        *late_core(2),
        bulk(0),
        bulk(1),
        late_to_chip(far),
        late_to_chip(near),
        *to_side(near),
    ):
        copy.wait_send()


def local(saved_modes, mode_gains):
    freqs, mode_count, pair, parts, comps, planes, rows, cols = saved_modes.shape
    freq_total = freqs * lax.axis_size("freq")
    factor = -2.0 / (freq_total * mode_count)
    band = rows // freq_total
    block_rows = band + 2 * MARGIN
    padded_planes = planes + 2 * PASSES
    f32 = jnp.float32
    return pl.pallas_call(
        functools.partial(gradient_kernel, lax.axis_size("space"), factor),
        out_shape=jax.ShapeDtypeStruct((planes, band, cols), f32),
        in_specs=[
            pl.BlockSpec(memory_space=pl.ANY),
            pl.BlockSpec(memory_space=pltpu.SMEM),
        ],
        out_specs=pl.BlockSpec(memory_space=pltpu.VMEM),
        scratch_shapes=[
            pltpu.VMEM((mode_count, pair, parts, comps, planes + 2, rows, cols), jnp.bfloat16),
            pltpu.VMEM((rows, rows), jnp.bfloat16),
            pltpu.VMEM((cols, cols), jnp.bfloat16),
            pltpu.VMEM((planes, rows, cols), f32),
            pltpu.VMEM((planes, rows + 2 * MARGIN, cols), f32),
            pltpu.VMEM((2, planes, block_rows, cols), f32),
            pltpu.VMEM((2, planes, block_rows, cols), f32),
            pltpu.VMEM((planes, band, cols), f32),
            pltpu.VMEM((planes, band, cols), f32),
            pltpu.VMEM((2, block_rows, cols), f32),
            pltpu.VMEM((2, 2, 2, block_rows, cols), f32),
            pltpu.VMEM((2, 2, block_rows, cols), f32),
            pltpu.VMEM((padded_planes, block_rows, cols), f32),
            pltpu.VMEM((padded_planes, block_rows, cols), f32),
            pltpu.VMEM((padded_planes, block_rows, cols), f32),
            pltpu.VMEM((padded_planes, block_rows, cols), f32),
            pltpu.VMEM((padded_planes, block_rows, cols), f32),
            pltpu.VMEM((padded_planes, block_rows, cols), f32),
            pltpu.SemaphoreType.DMA((mode_count,)),
            pltpu.SemaphoreType.DMA((2, 2, 2 * mode_count)),
            pltpu.SemaphoreType.DMA((2, 3, 2)),
            pltpu.SemaphoreType.DMA((2, 4)),
            pltpu.SemaphoreType.DMA((2, 2, 4)),
            pltpu.SemaphoreType.REGULAR,
            pltpu.SemaphoreType.REGULAR,
        ],
        compiler_params=pltpu.CompilerParams(
            collective_id=0, has_side_effects=True, vmem_limit_bytes=40 << 20
        ),
        name="gradient",
    )(saved_modes, mode_gains)


def solution(mesh):
    in_specs = (P("freq", None, None, None, None, "space", None, None), P("freq", None))
    out_specs = P("space", "freq", None)
    return jax.shard_map(local, mesh=mesh, in_specs=in_specs, out_specs=out_specs, check_vma=False)
```

```python
import functools

import jax
import jax.numpy as jnp
from jax import lax
from jax.experimental import pallas as pl
from jax.experimental.pallas import tpu as pltpu
from jax.sharding import PartitionSpec as P

AXIAL = 0.35
CROSS = 0.06
PASSES = 3
MARGIN = 4
LATE_CHUNKS = 2
BULK = (6, 3)
MESH = pl.DeviceIdType.MESH


def diff_matrices(count):
    row = lax.broadcasted_iota(jnp.int32, (count, count), 0)
    col = lax.broadcasted_iota(jnp.int32, (count, count), 1)
    upper = (col == row + 1).astype(jnp.float32)
    lower = (col + 1 == row).astype(jnp.float32)
    along_rows = (upper - lower).astype(jnp.bfloat16)
    along_cols = (lower - upper).astype(jnp.bfloat16)
    return along_rows, along_cols


def strain_parts(field, x, diff_y, diff_z):
    center = [field[c, x] for c in range(3)]
    after = [field[c, x + 1].astype(jnp.float32) for c in range(3)]
    before = [field[c, x - 1].astype(jnp.float32) for c in range(3)]
    dx = [after[c] - before[c] for c in range(3)]
    dy = [jnp.dot(diff_y, center[c], preferred_element_type=jnp.float32) for c in range(3)]
    dz = [jnp.dot(center[c], diff_z, preferred_element_type=jnp.float32) for c in range(3)]
    return (dx[0], dy[1], dz[2], dx[1] + dy[0], dx[2] + dz[0], dy[2] + dz[1])


def pair_term(forward, adjoint, x, diff_y, diff_z):
    eu = strain_parts(forward, x, diff_y, diff_z)
    ev = strain_parts(adjoint, x, diff_y, diff_z)
    straight = eu[0] * ev[0] + eu[1] * ev[1] + eu[2] * ev[2]
    shear = eu[3] * ev[3] + eu[4] * ev[4] + eu[5] * ev[5]
    return straight + 0.5 * shear


def gradient_kernel(
    space,
    factor,
    modes,
    gains,
    out,
    buf,
    ymat,
    zmat,
    acc,
    rows_out,
    from_core,
    chip_sum,
    smooth_sum,
    from_chip,
    late_chip,
    from_side,
    late_side,
    grid0,
    grid1,
    grid2,
    late0,
    late1,
    late2,
    load_sem,
    halo_sem,
    core_sem,
    chip_sem,
    side_sem,
    core_in,
    chip_in,
):
    mode_count = modes.shape[1]
    planes = modes.shape[5]
    rows = modes.shape[6]
    cols = modes.shape[7]
    chunks = 2 * mode_count
    inner = planes - 2
    band = out.shape[1]
    block_rows = band + 2 * MARGIN
    me = lax.axis_index("space")
    freq = lax.axis_index("freq")
    core = lax.rem(freq, 2)
    chip = freq // 2
    other_core = freq + 1 - 2 * core
    other_chip = lax.rem(freq + 2, 4)
    far = 1 - lax.rem(me, 2)
    near = 1 - far
    has_far = (me > 0) & (me < space - 1)

    def slab(side):
        return lax.rem(me + 1 - 2 * side + space, space)

    def send(src, dst, sems, index, freq_to, space_to):
        return pltpu.make_async_remote_copy(
            src_ref=src,
            dst_ref=dst,
            send_sem=sems.at[(0, *index)],
            recv_sem=sems.at[(1, *index)],
            device_id={"freq": freq_to, "space": space_to},
            device_id_type=MESH,
        )

    def load(m):
        return pltpu.make_async_copy(
            modes.at[0, m], buf.at[m, :, :, :, pl.ds(1, planes)], load_sem.at[m]
        )

    def halo(c, side):
        m, part = c // 2, lax.rem(c, 2)
        return send(
            modes.at[0, m, :, part, :, (planes - 1) * (1 - side)],
            buf.at[m, :, part, :, (planes + 1) * side],
            halo_sem,
            (side, c),
            freq,
            slab(side),
        )

    def block(half, owner_core):
        start = pl.multiple_of((2 * half + owner_core) * band, 8)
        return pl.ds(start, block_rows)

    def to_core(stage, first, count):
        return [
            send(
                rows_out.at[pl.ds(first, count), block(half, 1 - core)],
                from_core.at[half, pl.ds(first, count)],
                core_sem,
                (stage, half),
                other_core,
                me,
            )
            for half in range(2)
        ]

    def bulk(group):
        first = sum(BULK[:group])
        count = (*BULK, planes - sum(BULK))[group]
        return send(
            smooth_sum.at[pl.ds(first, count)],
            from_chip.at[pl.ds(first, count)],
            chip_sem,
            (group,),
            other_chip,
            me,
        )

    def late_to_chip(side):
        return send(
            chip_sum.at[1 - chip, inner + side],
            late_chip.at[side],
            chip_sem,
            (3 + side,),
            other_chip,
            me,
        )

    def early_to_side(side, half):
        return send(
            chip_sum.at[half, pl.ds((inner - 2) * (1 - side), 2)],
            from_side.at[side, half],
            side_sem,
            (side, half),
            other_chip,
            slab(side),
        )

    def late_to_side(side, same):
        half, target_freq = (chip, freq) if same else (1 - chip, other_chip)
        return send(
            chip_sum.at[half, inner + side],
            late_side.at[side, same],
            side_sem,
            (side, 2 + same),
            target_freq,
            slab(side),
        )

    def shift_rows(place):
        edge = jnp.zeros((MARGIN, cols), jnp.float32)
        rows_out[place] = jnp.concatenate([edge, acc[place], edge], axis=0)

    def add_cores(place):
        for half in range(2):
            chip_sum[half, place] = rows_out[place, block(half, core)] + from_core[half, place]

    load(0).start()
    barrier = pltpu.get_barrier_semaphore()

    def greet(freq_to, space_to):
        pl.semaphore_signal(
            barrier, inc=1, device_id={"freq": freq_to, "space": space_to}, device_id_type=MESH
        )

    @pl.when(has_far)
    def _():
        greet(freq, slab(far))

    greet(freq, slab(near))

    @pl.when(core == 0)
    def _():
        greet(other_core, me)

    @pl.when(chip == 0)
    def _():
        greet(other_chip, me)

    pl.semaphore_wait(barrier, jnp.where(has_far, 2, 1) + core + chip)

    def start_far(c):
        @pl.when(has_far)
        def _():
            halo(c, far).start()

    def start_halos(first, last):
        @pl.loop(first, last)
        def _(c):
            start_far(c + 1)
            halo(c, near).start()

    start_far(0)
    start_halos(0, chunks - LATE_CHUNKS)

    def answer(sem, freq_to):
        pl.semaphore_signal(
            sem, inc=1, device_id={"freq": freq_to, "space": me}, device_id_type=MESH
        )

    @pl.when(core == 1)
    def _():
        answer(core_in, other_core)

    @pl.when(chip == 1)
    def _():
        answer(chip_in, other_chip)

    @pl.loop(1, mode_count)
    def _(m):
        load(m).start()

    diff_y, diff_z = diff_matrices(rows)
    ymat[...] = diff_y
    zmat[...] = diff_z
    acc[...] = jnp.zeros_like(acc)

    @pl.when(jnp.logical_not(has_far))
    def _():
        @pl.loop(0, mode_count)
        def _(m):
            outer = buf.at[m, :, :, :, (planes + 1) * (1 - far)]
            outer[...] = jnp.zeros(outer.shape, outer.dtype)

        for landing in (from_side, late_side):
            missing = landing.at[1 - far]
            missing[...] = jnp.zeros(missing.shape, missing.dtype)

    def term(m, part, x):
        return pair_term(buf.at[m, 0, part], buf.at[m, 1, part], x, ymat[...], zmat[...])

    @pl.loop(0, mode_count)
    def _(m):
        load(m).wait()
        weight = gains[0, m] * (0.25 * factor)

        @pl.loop(0, inner)
        def _(q):
            acc[q] += weight * (term(m, 0, q + 2) + term(m, 1, q + 2))

    @pl.loop(0, inner)
    def _(q):
        shift_rows(q)

    @pl.when(core == 0)
    def _():
        pl.semaphore_wait(core_in, 1)

    @pl.when(chip == 0)
    def _():
        pl.semaphore_wait(chip_in, 1)
        answer(chip_in, other_chip)

    early = to_core(0, 0, inner)
    for copy in early:
        copy.start()
    for copy in early:
        copy.wait_recv()

    @pl.loop(0, inner)
    def _(q):
        add_cores(q)

    @pl.when(chip == 1)
    def _():
        pl.semaphore_wait(chip_in, 1)

    @pl.when(has_far)
    def _():
        for half in range(2):
            early_to_side(far, half).start()

    for half in range(2):
        early_to_side(near, half).start()

    row = lax.broadcasted_iota(jnp.int32, (block_rows, cols), 0) - MARGIN
    col = lax.broadcasted_iota(jnp.int32, (block_rows, cols), 1)
    not_first = (col > 0).astype(jnp.float32)
    not_last = (col < cols - 1).astype(jnp.float32)

    def smoothed(source, i):
        center = source[i]
        axial = source[i + 1] + source[i - 1] - 2.0 * center
        cross = (
            pltpu.roll(center, 1, 0)
            + pltpu.roll(center, block_rows - 1, 0)
            + pltpu.roll(center, 1, 1) * not_first
            + pltpu.roll(center, cols - 1, 1) * not_last
            - 4.0 * center
        )
        return center + AXIAL * axial + CROSS * cross

    def one_pass(source, target, half, first, count, width):
        at_row = row + (2 * half + core) * band
        inside = ((at_row >= 0) & (at_row < rows)).astype(jnp.float32)

        @pl.loop(0, count // width)
        def _(k):
            for j in range(width):
                i = first + k * width + j
                place = me * planes - PASSES + i
                kept = jnp.where((place >= 0) & (place < space * planes), 1.0, 0.0)
                target[i] = smoothed(source, i) * (inside * kept.astype(jnp.float32))

    def last_pass(source, first, count, width, store):
        @pl.loop(0, count // width)
        def _(k):
            for j in range(width):
                i = first + k * width + j
                store(i - PASSES, smoothed(source, i)[MARGIN : MARGIN + band])

    def smooth_early(half, store):
        @pl.loop(0, inner)
        def _(q):
            grid0[q + PASSES + 1] = chip_sum[half, q]

        for i in range(2):
            grid0[i] = from_side[0, half, i]
            grid0[PASSES + planes + 1 + i] = from_side[1, half, i]
        one_pass(grid0, grid1, half, 1, planes + 4, 2)
        one_pass(grid1, grid2, half, 2, planes + 2, 2)
        last_pass(grid2, 3, planes, 2, store)

    def keep(p, value):
        out[p] = value

    def pass_on(p, value):
        smooth_sum[p] = value

    for edge in (grid0, late0, late1, late2):
        edge[...] = jnp.zeros_like(edge)

    @pl.when(has_far)
    def _():
        for half in range(2):
            early_to_side(1 - far, half).wait_recv()

    for half in range(2):
        early_to_side(1 - near, half).wait_recv()
    smooth_early(1 - chip, pass_on)
    bulk(0).start()
    start_halos(chunks - LATE_CHUNKS, chunks - 1)
    halo(chunks - 1, near).start()
    bulk(1).start()
    smooth_early(chip, keep)

    far_place = inner + far
    near_place = inner + near

    def late_core(stage):
        return to_core(stage, far_place if stage == 1 else near_place, 1)

    @pl.loop(0, 2 * chunks)
    def _(i):
        turn = (i == 0) | ((lax.rem(i, 2) == 1) & (i < 2 * chunks - 1))
        c = (i + 1) // 2 - jnp.where(turn, 0, 1)
        side = jnp.where(turn, far, near)
        m, part = c // 2, lax.rem(c, 2)

        @pl.when((side == near) | has_far)
        def _():
            halo(c, 1 - side).wait_recv()

        weight = gains[0, m] * (0.25 * factor)
        acc[inner + side] += weight * term(m, part, planes - (planes - 1) * side)

        @pl.when(i == 2 * chunks - 3)
        def _():
            shift_rows(far_place)
            for copy in late_core(1):
                copy.start()

        @pl.when(i == 2 * chunks - 2)
        def _():
            for copy in late_core(1):
                copy.wait_recv()
            add_cores(far_place)

            @pl.when(has_far)
            def _():
                for same in (1, 0):
                    late_to_side(far, same).start()

            late_to_chip(far).start()
            bulk(2).start()

    shift_rows(near_place)
    for copy in late_core(2):
        copy.start()
    for copy in late_core(2):
        copy.wait_recv()
    add_cores(near_place)
    late_to_chip(near).start()
    for same in (1, 0):
        late_to_side(near, same).start()

    for group in range(3):
        bulk(group).wait_recv()

    @pl.loop(0, planes)
    def _(p):
        out[p] += from_chip[p]

    def add_late(p, value):
        out[p] += value

    def smooth_late(side):
        late0[PASSES + (planes - 1) * (1 - side)] = chip_sum[chip, inner + side] + late_chip[side]
        late0[PASSES - 1 + (planes + 1) * (1 - side)] = (
            late_side[1 - side, 0] + late_side[1 - side, 1]
        )
        start = [(planes + 1 - step) * (1 - side) + (1 + step) * side for step in range(PASSES)]
        one_pass(late0, late1, chip, start[0], 4, 4)
        one_pass(late1, late2, chip, start[1], 4, 4)
        last_pass(late2, start[2], 4, 4, add_late)

    late_to_chip(far).wait_recv()

    @pl.when(has_far)
    def _():
        for same in (1, 0):
            late_to_side(1 - far, same).wait_recv()

    smooth_late(far)
    late_to_chip(near).wait_recv()
    for same in (1, 0):
        late_to_side(1 - near, same).wait_recv()
    smooth_late(near)

    @pl.loop(0, chunks)
    def _(c):
        @pl.when(has_far)
        def _():
            halo(c, far).wait_send()

        halo(c, near).wait_send()

    def to_side(side):
        return (
            *(early_to_side(side, half) for half in range(2)),
            *(late_to_side(side, same) for same in (1, 0)),
        )

    @pl.when(has_far)
    def _():
        for copy in to_side(far):
            copy.wait_send()

    for copy in (
        *early,
        *late_core(1),
        *late_core(2),
        *(bulk(group) for group in range(3)),
        late_to_chip(far),
        late_to_chip(near),
        *to_side(near),
    ):
        copy.wait_send()


def local(saved_modes, mode_gains):
    freqs, mode_count, pair, parts, comps, planes, rows, cols = saved_modes.shape
    freq_total = freqs * lax.axis_size("freq")
    factor = -2.0 / (freq_total * mode_count)
    band = rows // freq_total
    block_rows = band + 2 * MARGIN
    padded_planes = planes + 2 * PASSES
    f32 = jnp.float32
    return pl.pallas_call(
        functools.partial(gradient_kernel, lax.axis_size("space"), factor),
        out_shape=jax.ShapeDtypeStruct((planes, band, cols), f32),
        in_specs=[
            pl.BlockSpec(memory_space=pl.ANY),
            pl.BlockSpec(memory_space=pltpu.SMEM),
        ],
        out_specs=pl.BlockSpec(memory_space=pltpu.VMEM),
        scratch_shapes=[
            pltpu.VMEM((mode_count, pair, parts, comps, planes + 2, rows, cols), jnp.bfloat16),
            pltpu.VMEM((rows, rows), jnp.bfloat16),
            pltpu.VMEM((cols, cols), jnp.bfloat16),
            pltpu.VMEM((planes, rows, cols), f32),
            pltpu.VMEM((planes, rows + 2 * MARGIN, cols), f32),
            pltpu.VMEM((2, planes, block_rows, cols), f32),
            pltpu.VMEM((2, planes, block_rows, cols), f32),
            pltpu.VMEM((planes, band, cols), f32),
            pltpu.VMEM((planes, band, cols), f32),
            pltpu.VMEM((2, block_rows, cols), f32),
            pltpu.VMEM((2, 2, 2, block_rows, cols), f32),
            pltpu.VMEM((2, 2, block_rows, cols), f32),
            pltpu.VMEM((padded_planes, block_rows, cols), f32),
            pltpu.VMEM((padded_planes, block_rows, cols), f32),
            pltpu.VMEM((padded_planes, block_rows, cols), f32),
            pltpu.VMEM((padded_planes, block_rows, cols), f32),
            pltpu.VMEM((padded_planes, block_rows, cols), f32),
            pltpu.VMEM((padded_planes, block_rows, cols), f32),
            pltpu.SemaphoreType.DMA((mode_count,)),
            pltpu.SemaphoreType.DMA((2, 2, 2 * mode_count)),
            pltpu.SemaphoreType.DMA((2, 3, 2)),
            pltpu.SemaphoreType.DMA((2, 5)),
            pltpu.SemaphoreType.DMA((2, 2, 4)),
            pltpu.SemaphoreType.REGULAR,
            pltpu.SemaphoreType.REGULAR,
        ],
        compiler_params=pltpu.CompilerParams(
            collective_id=0, has_side_effects=True, vmem_limit_bytes=40 << 20
        ),
        name="gradient",
    )(saved_modes, mode_gains)


def solution(mesh):
    in_specs = (P("freq", None, None, None, None, "space", None, None), P("freq", None))
    out_specs = P("space", "freq", None)
    return jax.shard_map(local, mesh=mesh, in_specs=in_specs, out_specs=out_specs, check_vma=False)
```

```python
import functools

import jax
import jax.numpy as jnp
from jax import lax
from jax.experimental import pallas as pl
from jax.experimental.pallas import tpu as pltpu
from jax.sharding import PartitionSpec as P

AXIAL = 0.35
CROSS = 0.06
PASSES = 3
MARGIN = 4
LATE_CHUNKS = 2
BULK = (6, 3, 4)
MESH = pl.DeviceIdType.MESH


def diff_matrices(count):
    row = lax.broadcasted_iota(jnp.int32, (count, count), 0)
    col = lax.broadcasted_iota(jnp.int32, (count, count), 1)
    upper = (col == row + 1).astype(jnp.float32)
    lower = (col + 1 == row).astype(jnp.float32)
    along_rows = (upper - lower).astype(jnp.bfloat16)
    along_cols = (lower - upper).astype(jnp.bfloat16)
    return along_rows, along_cols


def strain_parts(field, x, diff_y, diff_z):
    center = [field[c, x] for c in range(3)]
    after = [field[c, x + 1].astype(jnp.float32) for c in range(3)]
    before = [field[c, x - 1].astype(jnp.float32) for c in range(3)]
    dx = [after[c] - before[c] for c in range(3)]
    dy = [jnp.dot(diff_y, center[c], preferred_element_type=jnp.float32) for c in range(3)]
    dz = [jnp.dot(center[c], diff_z, preferred_element_type=jnp.float32) for c in range(3)]
    return (dx[0], dy[1], dz[2], dx[1] + dy[0], dx[2] + dz[0], dy[2] + dz[1])


def pair_term(forward, adjoint, x, diff_y, diff_z):
    eu = strain_parts(forward, x, diff_y, diff_z)
    ev = strain_parts(adjoint, x, diff_y, diff_z)
    straight = eu[0] * ev[0] + eu[1] * ev[1] + eu[2] * ev[2]
    shear = eu[3] * ev[3] + eu[4] * ev[4] + eu[5] * ev[5]
    return straight + 0.5 * shear


def gradient_kernel(
    space,
    factor,
    modes,
    gains,
    out,
    buf,
    ymat,
    zmat,
    acc,
    rows_out,
    from_core,
    chip_sum,
    smooth_sum,
    from_chip,
    late_chip,
    from_side,
    late_side,
    grid0,
    grid1,
    grid2,
    late0,
    late1,
    late2,
    load_sem,
    halo_sem,
    core_sem,
    chip_sem,
    side_sem,
    core_in,
    chip_in,
):
    mode_count = modes.shape[1]
    planes = modes.shape[5]
    rows = modes.shape[6]
    cols = modes.shape[7]
    chunks = 2 * mode_count
    inner = planes - 2
    band = out.shape[1]
    block_rows = band + 2 * MARGIN
    me = lax.axis_index("space")
    freq = lax.axis_index("freq")
    core = lax.rem(freq, 2)
    chip = freq // 2
    other_core = freq + 1 - 2 * core
    other_chip = lax.rem(freq + 2, 4)
    far = 1 - lax.rem(me, 2)
    near = 1 - far
    has_far = (me > 0) & (me < space - 1)

    def slab(side):
        return lax.rem(me + 1 - 2 * side + space, space)

    def send(src, dst, sems, index, freq_to, space_to):
        return pltpu.make_async_remote_copy(
            src_ref=src,
            dst_ref=dst,
            send_sem=sems.at[(0, *index)],
            recv_sem=sems.at[(1, *index)],
            device_id={"freq": freq_to, "space": space_to},
            device_id_type=MESH,
        )

    def load(m):
        return pltpu.make_async_copy(
            modes.at[0, m], buf.at[m, :, :, :, pl.ds(1, planes)], load_sem.at[m]
        )

    def halo(c, side):
        m, part = c // 2, lax.rem(c, 2)
        return send(
            modes.at[0, m, :, part, :, (planes - 1) * (1 - side)],
            buf.at[m, :, part, :, (planes + 1) * side],
            halo_sem,
            (side, c),
            freq,
            slab(side),
        )

    def block(half, owner_core):
        start = pl.multiple_of((2 * half + owner_core) * band, 8)
        return pl.ds(start, block_rows)

    def to_core(stage, first, count):
        return [
            send(
                rows_out.at[pl.ds(first, count), block(half, 1 - core)],
                from_core.at[half, pl.ds(first, count)],
                core_sem,
                (stage, half),
                other_core,
                me,
            )
            for half in range(2)
        ]

    def bulk(group):
        first = sum(BULK[:group])
        count = (*BULK, planes - sum(BULK))[group]
        return send(
            smooth_sum.at[pl.ds(first, count)],
            from_chip.at[pl.ds(first, count)],
            chip_sem,
            (group,),
            other_chip,
            me,
        )

    def late_to_chip(side):
        return send(
            chip_sum.at[1 - chip, inner + side],
            late_chip.at[side],
            chip_sem,
            (4 + side,),
            other_chip,
            me,
        )

    def early_to_side(side, half):
        return send(
            chip_sum.at[half, pl.ds((inner - 2) * (1 - side), 2)],
            from_side.at[side, half],
            side_sem,
            (side, half),
            other_chip,
            slab(side),
        )

    def late_to_side(side, same):
        half, target_freq = (chip, freq) if same else (1 - chip, other_chip)
        return send(
            chip_sum.at[half, inner + side],
            late_side.at[side, same],
            side_sem,
            (side, 2 + same),
            target_freq,
            slab(side),
        )

    def shift_rows(place):
        edge = jnp.zeros((MARGIN, cols), jnp.float32)
        rows_out[place] = jnp.concatenate([edge, acc[place], edge], axis=0)

    def add_cores(place):
        for half in range(2):
            chip_sum[half, place] = rows_out[place, block(half, core)] + from_core[half, place]

    load(0).start()
    barrier = pltpu.get_barrier_semaphore()

    def greet(freq_to, space_to):
        pl.semaphore_signal(
            barrier, inc=1, device_id={"freq": freq_to, "space": space_to}, device_id_type=MESH
        )

    @pl.when(has_far)
    def _():
        greet(freq, slab(far))

    greet(freq, slab(near))

    @pl.when(core == 0)
    def _():
        greet(other_core, me)

    @pl.when(chip == 0)
    def _():
        greet(other_chip, me)

    pl.semaphore_wait(barrier, jnp.where(has_far, 2, 1) + core + chip)

    def start_far(c):
        @pl.when(has_far)
        def _():
            halo(c, far).start()

    def start_halos(first, last):
        @pl.loop(first, last)
        def _(c):
            start_far(c + 1)
            halo(c, near).start()

    start_far(0)
    start_halos(0, chunks - LATE_CHUNKS)

    def answer(sem, freq_to):
        pl.semaphore_signal(
            sem, inc=1, device_id={"freq": freq_to, "space": me}, device_id_type=MESH
        )

    @pl.when(core == 1)
    def _():
        answer(core_in, other_core)

    @pl.when(chip == 1)
    def _():
        answer(chip_in, other_chip)

    @pl.loop(1, mode_count)
    def _(m):
        load(m).start()

    diff_y, diff_z = diff_matrices(rows)
    ymat[...] = diff_y
    zmat[...] = diff_z
    acc[...] = jnp.zeros_like(acc)

    @pl.when(jnp.logical_not(has_far))
    def _():
        @pl.loop(0, mode_count)
        def _(m):
            outer = buf.at[m, :, :, :, (planes + 1) * (1 - far)]
            outer[...] = jnp.zeros(outer.shape, outer.dtype)

        for landing in (from_side, late_side):
            missing = landing.at[1 - far]
            missing[...] = jnp.zeros(missing.shape, missing.dtype)

    def term(m, part, x):
        return pair_term(buf.at[m, 0, part], buf.at[m, 1, part], x, ymat[...], zmat[...])

    @pl.loop(0, mode_count)
    def _(m):
        load(m).wait()
        weight = gains[0, m] * (0.25 * factor)

        @pl.loop(0, inner)
        def _(q):
            acc[q] += weight * (term(m, 0, q + 2) + term(m, 1, q + 2))

    @pl.loop(0, inner)
    def _(q):
        shift_rows(q)

    @pl.when(core == 0)
    def _():
        pl.semaphore_wait(core_in, 1)

    @pl.when(chip == 0)
    def _():
        pl.semaphore_wait(chip_in, 1)
        answer(chip_in, other_chip)

    early = to_core(0, 0, inner)
    for copy in early:
        copy.start()
    for copy in early:
        copy.wait_recv()

    @pl.loop(0, inner)
    def _(q):
        add_cores(q)

    @pl.when(chip == 1)
    def _():
        pl.semaphore_wait(chip_in, 1)

    @pl.when(has_far)
    def _():
        for half in range(2):
            early_to_side(far, half).start()

    for half in range(2):
        early_to_side(near, half).start()

    row = lax.broadcasted_iota(jnp.int32, (block_rows, cols), 0) - MARGIN
    col = lax.broadcasted_iota(jnp.int32, (block_rows, cols), 1)
    not_first = (col > 0).astype(jnp.float32)
    not_last = (col < cols - 1).astype(jnp.float32)

    def smoothed(source, i):
        center = source[i]
        axial = source[i + 1] + source[i - 1] - 2.0 * center
        cross = (
            pltpu.roll(center, 1, 0)
            + pltpu.roll(center, block_rows - 1, 0)
            + pltpu.roll(center, 1, 1) * not_first
            + pltpu.roll(center, cols - 1, 1) * not_last
            - 4.0 * center
        )
        return center + AXIAL * axial + CROSS * cross

    def one_pass(source, target, half, first, count, width):
        at_row = row + (2 * half + core) * band
        inside = ((at_row >= 0) & (at_row < rows)).astype(jnp.float32)

        @pl.loop(0, count // width)
        def _(k):
            for j in range(width):
                i = first + k * width + j
                place = me * planes - PASSES + i
                kept = jnp.where((place >= 0) & (place < space * planes), 1.0, 0.0)
                target[i] = smoothed(source, i) * (inside * kept.astype(jnp.float32))

    def last_pass(source, first, count, width, store):
        @pl.loop(0, count // width)
        def _(k):
            for j in range(width):
                i = first + k * width + j
                store(i - PASSES, smoothed(source, i)[MARGIN : MARGIN + band])

    def smooth_early(half, store):
        @pl.loop(0, inner)
        def _(q):
            grid0[q + PASSES + 1] = chip_sum[half, q]

        for i in range(2):
            grid0[i] = from_side[0, half, i]
            grid0[PASSES + planes + 1 + i] = from_side[1, half, i]
        one_pass(grid0, grid1, half, 1, planes + 4, 2)
        one_pass(grid1, grid2, half, 2, planes + 2, 2)
        last_pass(grid2, 3, planes, 2, store)

    def keep(p, value):
        out[p] = value

    def pass_on(p, value):
        smooth_sum[p] = value

    for edge in (grid0, late0, late1, late2):
        edge[...] = jnp.zeros_like(edge)

    @pl.when(has_far)
    def _():
        for half in range(2):
            early_to_side(1 - far, half).wait_recv()

    for half in range(2):
        early_to_side(1 - near, half).wait_recv()
    smooth_early(1 - chip, pass_on)
    bulk(0).start()
    start_halos(chunks - LATE_CHUNKS, chunks - 1)
    halo(chunks - 1, near).start()
    bulk(1).start()
    smooth_early(chip, keep)

    far_place = inner + far
    near_place = inner + near

    def late_core(stage):
        return to_core(stage, far_place if stage == 1 else near_place, 1)

    @pl.loop(0, 2 * chunks)
    def _(i):
        turn = (i == 0) | ((lax.rem(i, 2) == 1) & (i < 2 * chunks - 1))
        c = (i + 1) // 2 - jnp.where(turn, 0, 1)
        side = jnp.where(turn, far, near)
        m, part = c // 2, lax.rem(c, 2)

        @pl.when((side == near) | has_far)
        def _():
            halo(c, 1 - side).wait_recv()

        weight = gains[0, m] * (0.25 * factor)
        acc[inner + side] += weight * term(m, part, planes - (planes - 1) * side)

        @pl.when(i == 2 * chunks - 3)
        def _():
            shift_rows(far_place)
            for copy in late_core(1):
                copy.start()

        @pl.when(i == 2 * chunks - 2)
        def _():
            for copy in late_core(1):
                copy.wait_recv()
            add_cores(far_place)

            @pl.when(has_far)
            def _():
                for same in (1, 0):
                    late_to_side(far, same).start()

            late_to_chip(far).start()
            bulk(2).start()

    shift_rows(near_place)
    for copy in late_core(2):
        copy.start()
    for copy in late_core(2):
        copy.wait_recv()
    add_cores(near_place)
    late_to_chip(near).start()
    for same in (1, 0):
        late_to_side(near, same).start()
    bulk(3).start()

    def add_bulk(first, last):
        @pl.loop(first, last)
        def _(p):
            out[p] += from_chip[p]

    for group in range(3):
        bulk(group).wait_recv()
    add_bulk(0, sum(BULK))

    def add_late(p, value):
        out[p] += value

    def smooth_late(side):
        late0[PASSES + (planes - 1) * (1 - side)] = chip_sum[chip, inner + side] + late_chip[side]
        late0[PASSES - 1 + (planes + 1) * (1 - side)] = (
            late_side[1 - side, 0] + late_side[1 - side, 1]
        )
        start = [(planes + 1 - step) * (1 - side) + (1 + step) * side for step in range(PASSES)]
        one_pass(late0, late1, chip, start[0], 4, 4)
        one_pass(late1, late2, chip, start[1], 4, 4)
        last_pass(late2, start[2], 4, 4, add_late)

    late_to_chip(far).wait_recv()

    @pl.when(has_far)
    def _():
        for same in (1, 0):
            late_to_side(1 - far, same).wait_recv()

    smooth_late(far)
    late_to_chip(near).wait_recv()
    for same in (1, 0):
        late_to_side(1 - near, same).wait_recv()
    smooth_late(near)
    bulk(3).wait_recv()
    add_bulk(sum(BULK), planes)

    @pl.loop(0, chunks)
    def _(c):
        @pl.when(has_far)
        def _():
            halo(c, far).wait_send()

        halo(c, near).wait_send()

    def to_side(side):
        return (
            *(early_to_side(side, half) for half in range(2)),
            *(late_to_side(side, same) for same in (1, 0)),
        )

    @pl.when(has_far)
    def _():
        for copy in to_side(far):
            copy.wait_send()

    for copy in (
        *early,
        *late_core(1),
        *late_core(2),
        *(bulk(group) for group in range(4)),
        late_to_chip(far),
        late_to_chip(near),
        *to_side(near),
    ):
        copy.wait_send()


def local(saved_modes, mode_gains):
    freqs, mode_count, pair, parts, comps, planes, rows, cols = saved_modes.shape
    freq_total = freqs * lax.axis_size("freq")
    factor = -2.0 / (freq_total * mode_count)
    band = rows // freq_total
    block_rows = band + 2 * MARGIN
    padded_planes = planes + 2 * PASSES
    f32 = jnp.float32
    return pl.pallas_call(
        functools.partial(gradient_kernel, lax.axis_size("space"), factor),
        out_shape=jax.ShapeDtypeStruct((planes, band, cols), f32),
        in_specs=[
            pl.BlockSpec(memory_space=pl.ANY),
            pl.BlockSpec(memory_space=pltpu.SMEM),
        ],
        out_specs=pl.BlockSpec(memory_space=pltpu.VMEM),
        scratch_shapes=[
            pltpu.VMEM((mode_count, pair, parts, comps, planes + 2, rows, cols), jnp.bfloat16),
            pltpu.VMEM((rows, rows), jnp.bfloat16),
            pltpu.VMEM((cols, cols), jnp.bfloat16),
            pltpu.VMEM((planes, rows, cols), f32),
            pltpu.VMEM((planes, rows + 2 * MARGIN, cols), f32),
            pltpu.VMEM((2, planes, block_rows, cols), f32),
            pltpu.VMEM((2, planes, block_rows, cols), f32),
            pltpu.VMEM((planes, band, cols), f32),
            pltpu.VMEM((planes, band, cols), f32),
            pltpu.VMEM((2, block_rows, cols), f32),
            pltpu.VMEM((2, 2, 2, block_rows, cols), f32),
            pltpu.VMEM((2, 2, block_rows, cols), f32),
            pltpu.VMEM((padded_planes, block_rows, cols), f32),
            pltpu.VMEM((padded_planes, block_rows, cols), f32),
            pltpu.VMEM((padded_planes, block_rows, cols), f32),
            pltpu.VMEM((padded_planes, block_rows, cols), f32),
            pltpu.VMEM((padded_planes, block_rows, cols), f32),
            pltpu.VMEM((padded_planes, block_rows, cols), f32),
            pltpu.SemaphoreType.DMA((mode_count,)),
            pltpu.SemaphoreType.DMA((2, 2, 2 * mode_count)),
            pltpu.SemaphoreType.DMA((2, 3, 2)),
            pltpu.SemaphoreType.DMA((2, 6)),
            pltpu.SemaphoreType.DMA((2, 2, 4)),
            pltpu.SemaphoreType.REGULAR,
            pltpu.SemaphoreType.REGULAR,
        ],
        compiler_params=pltpu.CompilerParams(
            collective_id=0, has_side_effects=True, vmem_limit_bytes=40 << 20
        ),
        name="gradient",
    )(saved_modes, mode_gains)


def solution(mesh):
    in_specs = (P("freq", None, None, None, None, "space", None, None), P("freq", None))
    out_specs = P("space", "freq", None)
    return jax.shard_map(local, mesh=mesh, in_specs=in_specs, out_specs=out_specs, check_vma=False)
```

```python
import functools

import jax
import jax.numpy as jnp
from jax import lax
from jax.experimental import pallas as pl
from jax.experimental.pallas import tpu as pltpu
from jax.sharding import PartitionSpec as P

AXIAL = 0.35
CROSS = 0.06
PASSES = 3
MARGIN = 4
LATE_CHUNKS = 2
BULK = (5, 3, 4)
MESH = pl.DeviceIdType.MESH


def diff_matrices(count):
    row = lax.broadcasted_iota(jnp.int32, (count, count), 0)
    col = lax.broadcasted_iota(jnp.int32, (count, count), 1)
    upper = (col == row + 1).astype(jnp.float32)
    lower = (col + 1 == row).astype(jnp.float32)
    along_rows = (upper - lower).astype(jnp.bfloat16)
    along_cols = (lower - upper).astype(jnp.bfloat16)
    return along_rows, along_cols


def strain_parts(field, x, diff_y, diff_z):
    center = [field[c, x] for c in range(3)]
    after = [field[c, x + 1].astype(jnp.float32) for c in range(3)]
    before = [field[c, x - 1].astype(jnp.float32) for c in range(3)]
    dx = [after[c] - before[c] for c in range(3)]
    dy = [jnp.dot(diff_y, center[c], preferred_element_type=jnp.float32) for c in range(3)]
    dz = [jnp.dot(center[c], diff_z, preferred_element_type=jnp.float32) for c in range(3)]
    return (dx[0], dy[1], dz[2], dx[1] + dy[0], dx[2] + dz[0], dy[2] + dz[1])


def pair_term(forward, adjoint, x, diff_y, diff_z):
    eu = strain_parts(forward, x, diff_y, diff_z)
    ev = strain_parts(adjoint, x, diff_y, diff_z)
    straight = eu[0] * ev[0] + eu[1] * ev[1] + eu[2] * ev[2]
    shear = eu[3] * ev[3] + eu[4] * ev[4] + eu[5] * ev[5]
    return straight + 0.5 * shear


def gradient_kernel(
    space,
    factor,
    modes,
    gains,
    out,
    buf,
    ymat,
    zmat,
    acc,
    rows_out,
    from_core,
    chip_sum,
    smooth_sum,
    from_chip,
    late_chip,
    from_side,
    late_side,
    grid0,
    grid1,
    grid2,
    late0,
    late1,
    late2,
    load_sem,
    halo_sem,
    core_sem,
    chip_sem,
    side_sem,
    core_in,
    chip_in,
):
    mode_count = modes.shape[1]
    planes = modes.shape[5]
    rows = modes.shape[6]
    cols = modes.shape[7]
    chunks = 2 * mode_count
    inner = planes - 2
    band = out.shape[1]
    block_rows = band + 2 * MARGIN
    me = lax.axis_index("space")
    freq = lax.axis_index("freq")
    core = lax.rem(freq, 2)
    chip = freq // 2
    other_core = freq + 1 - 2 * core
    other_chip = lax.rem(freq + 2, 4)
    far = 1 - lax.rem(me, 2)
    near = 1 - far
    has_far = (me > 0) & (me < space - 1)

    def slab(side):
        return lax.rem(me + 1 - 2 * side + space, space)

    def send(src, dst, sems, index, freq_to, space_to):
        return pltpu.make_async_remote_copy(
            src_ref=src,
            dst_ref=dst,
            send_sem=sems.at[(0, *index)],
            recv_sem=sems.at[(1, *index)],
            device_id={"freq": freq_to, "space": space_to},
            device_id_type=MESH,
        )

    def load(m):
        return pltpu.make_async_copy(
            modes.at[0, m], buf.at[m, :, :, :, pl.ds(1, planes)], load_sem.at[m]
        )

    def halo(c, side):
        m, part = c // 2, lax.rem(c, 2)
        return send(
            modes.at[0, m, :, part, :, (planes - 1) * (1 - side)],
            buf.at[m, :, part, :, (planes + 1) * side],
            halo_sem,
            (side, c),
            freq,
            slab(side),
        )

    def block(half, owner_core):
        start = pl.multiple_of((2 * half + owner_core) * band, 8)
        return pl.ds(start, block_rows)

    def to_core(stage, first, count):
        return [
            send(
                rows_out.at[pl.ds(first, count), block(half, 1 - core)],
                from_core.at[half, pl.ds(first, count)],
                core_sem,
                (stage, half),
                other_core,
                me,
            )
            for half in range(2)
        ]

    def bulk(group):
        first = sum(BULK[:group])
        count = (*BULK, planes - sum(BULK))[group]
        return send(
            smooth_sum.at[pl.ds(first, count)],
            from_chip.at[pl.ds(first, count)],
            chip_sem,
            (group,),
            other_chip,
            me,
        )

    def late_to_chip(side):
        return send(
            chip_sum.at[1 - chip, inner + side],
            late_chip.at[side],
            chip_sem,
            (4 + side,),
            other_chip,
            me,
        )

    def early_to_side(side, half):
        return send(
            chip_sum.at[half, pl.ds((inner - 2) * (1 - side), 2)],
            from_side.at[side, half],
            side_sem,
            (side, half),
            other_chip,
            slab(side),
        )

    def late_to_side(side, same):
        half, target_freq = (chip, freq) if same else (1 - chip, other_chip)
        return send(
            chip_sum.at[half, inner + side],
            late_side.at[side, same],
            side_sem,
            (side, 2 + same),
            target_freq,
            slab(side),
        )

    def shift_rows(place):
        edge = jnp.zeros((MARGIN, cols), jnp.float32)
        rows_out[place] = jnp.concatenate([edge, acc[place], edge], axis=0)

    def add_cores(place):
        for half in range(2):
            chip_sum[half, place] = rows_out[place, block(half, core)] + from_core[half, place]

    load(0).start()
    barrier = pltpu.get_barrier_semaphore()

    def greet(freq_to, space_to):
        pl.semaphore_signal(
            barrier, inc=1, device_id={"freq": freq_to, "space": space_to}, device_id_type=MESH
        )

    @pl.when(has_far)
    def _():
        greet(freq, slab(far))

    greet(freq, slab(near))

    @pl.when(core == 0)
    def _():
        greet(other_core, me)

    @pl.when(chip == 0)
    def _():
        greet(other_chip, me)

    pl.semaphore_wait(barrier, jnp.where(has_far, 2, 1) + core + chip)

    def start_far(c):
        @pl.when(has_far)
        def _():
            halo(c, far).start()

    def start_halos(first, last):
        @pl.loop(first, last)
        def _(c):
            start_far(c + 1)
            halo(c, near).start()

    start_far(0)
    start_halos(0, chunks - LATE_CHUNKS)

    def answer(sem, freq_to):
        pl.semaphore_signal(
            sem, inc=1, device_id={"freq": freq_to, "space": me}, device_id_type=MESH
        )

    @pl.when(core == 1)
    def _():
        answer(core_in, other_core)

    @pl.when(chip == 1)
    def _():
        answer(chip_in, other_chip)

    @pl.loop(1, mode_count)
    def _(m):
        load(m).start()

    diff_y, diff_z = diff_matrices(rows)
    ymat[...] = diff_y
    zmat[...] = diff_z
    acc[...] = jnp.zeros_like(acc)

    @pl.when(jnp.logical_not(has_far))
    def _():
        @pl.loop(0, mode_count)
        def _(m):
            outer = buf.at[m, :, :, :, (planes + 1) * (1 - far)]
            outer[...] = jnp.zeros(outer.shape, outer.dtype)

        for landing in (from_side, late_side):
            missing = landing.at[1 - far]
            missing[...] = jnp.zeros(missing.shape, missing.dtype)

    def term(m, part, x):
        return pair_term(buf.at[m, 0, part], buf.at[m, 1, part], x, ymat[...], zmat[...])

    @pl.loop(0, mode_count)
    def _(m):
        load(m).wait()
        weight = gains[0, m] * (0.25 * factor)

        @pl.loop(0, inner)
        def _(q):
            acc[q] += weight * (term(m, 0, q + 2) + term(m, 1, q + 2))

    @pl.loop(0, inner)
    def _(q):
        shift_rows(q)

    @pl.when(core == 0)
    def _():
        pl.semaphore_wait(core_in, 1)

    @pl.when(chip == 0)
    def _():
        pl.semaphore_wait(chip_in, 1)
        answer(chip_in, other_chip)

    early = to_core(0, 0, inner)
    for copy in early:
        copy.start()
    for copy in early:
        copy.wait_recv()

    @pl.loop(0, inner)
    def _(q):
        add_cores(q)

    @pl.when(chip == 1)
    def _():
        pl.semaphore_wait(chip_in, 1)

    @pl.when(has_far)
    def _():
        for half in range(2):
            early_to_side(far, half).start()

    for half in range(2):
        early_to_side(near, half).start()

    row = lax.broadcasted_iota(jnp.int32, (block_rows, cols), 0) - MARGIN
    col = lax.broadcasted_iota(jnp.int32, (block_rows, cols), 1)
    not_first = (col > 0).astype(jnp.float32)
    not_last = (col < cols - 1).astype(jnp.float32)

    def smoothed(source, i):
        center = source[i]
        axial = source[i + 1] + source[i - 1] - 2.0 * center
        cross = (
            pltpu.roll(center, 1, 0)
            + pltpu.roll(center, block_rows - 1, 0)
            + pltpu.roll(center, 1, 1) * not_first
            + pltpu.roll(center, cols - 1, 1) * not_last
            - 4.0 * center
        )
        return center + AXIAL * axial + CROSS * cross

    def one_pass(source, target, half, first, count, width):
        at_row = row + (2 * half + core) * band
        inside = ((at_row >= 0) & (at_row < rows)).astype(jnp.float32)

        @pl.loop(0, count // width)
        def _(k):
            for j in range(width):
                i = first + k * width + j
                place = me * planes - PASSES + i
                kept = jnp.where((place >= 0) & (place < space * planes), 1.0, 0.0)
                target[i] = smoothed(source, i) * (inside * kept.astype(jnp.float32))

    def last_pass(source, first, count, width, store):
        @pl.loop(0, count // width)
        def _(k):
            for j in range(width):
                i = first + k * width + j
                store(i - PASSES, smoothed(source, i)[MARGIN : MARGIN + band])

    def smooth_early(half, store):
        @pl.loop(0, inner)
        def _(q):
            grid0[q + PASSES + 1] = chip_sum[half, q]

        for i in range(2):
            grid0[i] = from_side[0, half, i]
            grid0[PASSES + planes + 1 + i] = from_side[1, half, i]
        one_pass(grid0, grid1, half, 1, planes + 4, 2)
        one_pass(grid1, grid2, half, 2, planes + 2, 2)
        last_pass(grid2, 3, planes, 2, store)

    def keep(p, value):
        out[p] = value

    def pass_on(p, value):
        smooth_sum[p] = value

    for edge in (grid0, late0, late1, late2):
        edge[...] = jnp.zeros_like(edge)

    @pl.when(has_far)
    def _():
        for half in range(2):
            early_to_side(1 - far, half).wait_recv()

    for half in range(2):
        early_to_side(1 - near, half).wait_recv()
    smooth_early(1 - chip, pass_on)
    bulk(0).start()
    start_halos(chunks - LATE_CHUNKS, chunks - 1)
    halo(chunks - 1, near).start()
    bulk(1).start()
    smooth_early(chip, keep)

    far_place = inner + far
    near_place = inner + near

    def late_core(stage):
        return to_core(stage, far_place if stage == 1 else near_place, 1)

    @pl.loop(0, 2 * chunks)
    def _(i):
        turn = (i == 0) | ((lax.rem(i, 2) == 1) & (i < 2 * chunks - 1))
        c = (i + 1) // 2 - jnp.where(turn, 0, 1)
        side = jnp.where(turn, far, near)
        m, part = c // 2, lax.rem(c, 2)

        @pl.when((side == near) | has_far)
        def _():
            halo(c, 1 - side).wait_recv()

        weight = gains[0, m] * (0.25 * factor)
        acc[inner + side] += weight * term(m, part, planes - (planes - 1) * side)

        @pl.when(i == 2 * chunks - 3)
        def _():
            shift_rows(far_place)
            for copy in late_core(1):
                copy.start()

        @pl.when(i == 2 * chunks - 2)
        def _():
            for copy in late_core(1):
                copy.wait_recv()
            add_cores(far_place)

            @pl.when(has_far)
            def _():
                for same in (1, 0):
                    late_to_side(far, same).start()

            late_to_chip(far).start()
            bulk(2).start()

    shift_rows(near_place)
    for copy in late_core(2):
        copy.start()
    for copy in late_core(2):
        copy.wait_recv()
    add_cores(near_place)
    late_to_chip(near).start()
    for same in (1, 0):
        late_to_side(near, same).start()
    bulk(3).start()

    def add_bulk(first, last):
        @pl.loop(first, last)
        def _(p):
            out[p] += from_chip[p]

    for group in range(3):
        bulk(group).wait_recv()
    add_bulk(0, sum(BULK))

    def add_late(p, value):
        out[p] += value

    def smooth_late(side):
        late0[PASSES + (planes - 1) * (1 - side)] = chip_sum[chip, inner + side] + late_chip[side]
        late0[PASSES - 1 + (planes + 1) * (1 - side)] = (
            late_side[1 - side, 0] + late_side[1 - side, 1]
        )
        start = [(planes + 1 - step) * (1 - side) + (1 + step) * side for step in range(PASSES)]
        one_pass(late0, late1, chip, start[0], 4, 4)
        one_pass(late1, late2, chip, start[1], 4, 4)
        last_pass(late2, start[2], 4, 4, add_late)

    late_to_chip(far).wait_recv()

    @pl.when(has_far)
    def _():
        for same in (1, 0):
            late_to_side(1 - far, same).wait_recv()

    smooth_late(far)
    late_to_chip(near).wait_recv()
    for same in (1, 0):
        late_to_side(1 - near, same).wait_recv()
    smooth_late(near)
    bulk(3).wait_recv()
    add_bulk(sum(BULK), planes)

    @pl.loop(0, chunks)
    def _(c):
        @pl.when(has_far)
        def _():
            halo(c, far).wait_send()

        halo(c, near).wait_send()

    def to_side(side):
        return (
            *(early_to_side(side, half) for half in range(2)),
            *(late_to_side(side, same) for same in (1, 0)),
        )

    @pl.when(has_far)
    def _():
        for copy in to_side(far):
            copy.wait_send()

    for copy in (
        *early,
        *late_core(1),
        *late_core(2),
        *(bulk(group) for group in range(4)),
        late_to_chip(far),
        late_to_chip(near),
        *to_side(near),
    ):
        copy.wait_send()


def local(saved_modes, mode_gains):
    freqs, mode_count, pair, parts, comps, planes, rows, cols = saved_modes.shape
    freq_total = freqs * lax.axis_size("freq")
    factor = -2.0 / (freq_total * mode_count)
    band = rows // freq_total
    block_rows = band + 2 * MARGIN
    padded_planes = planes + 2 * PASSES
    f32 = jnp.float32
    return pl.pallas_call(
        functools.partial(gradient_kernel, lax.axis_size("space"), factor),
        out_shape=jax.ShapeDtypeStruct((planes, band, cols), f32),
        in_specs=[
            pl.BlockSpec(memory_space=pl.ANY),
            pl.BlockSpec(memory_space=pltpu.SMEM),
        ],
        out_specs=pl.BlockSpec(memory_space=pltpu.VMEM),
        scratch_shapes=[
            pltpu.VMEM((mode_count, pair, parts, comps, planes + 2, rows, cols), jnp.bfloat16),
            pltpu.VMEM((rows, rows), jnp.bfloat16),
            pltpu.VMEM((cols, cols), jnp.bfloat16),
            pltpu.VMEM((planes, rows, cols), f32),
            pltpu.VMEM((planes, rows + 2 * MARGIN, cols), f32),
            pltpu.VMEM((2, planes, block_rows, cols), f32),
            pltpu.VMEM((2, planes, block_rows, cols), f32),
            pltpu.VMEM((planes, band, cols), f32),
            pltpu.VMEM((planes, band, cols), f32),
            pltpu.VMEM((2, block_rows, cols), f32),
            pltpu.VMEM((2, 2, 2, block_rows, cols), f32),
            pltpu.VMEM((2, 2, block_rows, cols), f32),
            pltpu.VMEM((padded_planes, block_rows, cols), f32),
            pltpu.VMEM((padded_planes, block_rows, cols), f32),
            pltpu.VMEM((padded_planes, block_rows, cols), f32),
            pltpu.VMEM((padded_planes, block_rows, cols), f32),
            pltpu.VMEM((padded_planes, block_rows, cols), f32),
            pltpu.VMEM((padded_planes, block_rows, cols), f32),
            pltpu.SemaphoreType.DMA((mode_count,)),
            pltpu.SemaphoreType.DMA((2, 2, 2 * mode_count)),
            pltpu.SemaphoreType.DMA((2, 3, 2)),
            pltpu.SemaphoreType.DMA((2, 6)),
            pltpu.SemaphoreType.DMA((2, 2, 4)),
            pltpu.SemaphoreType.REGULAR,
            pltpu.SemaphoreType.REGULAR,
        ],
        compiler_params=pltpu.CompilerParams(
            collective_id=0, has_side_effects=True, vmem_limit_bytes=40 << 20
        ),
        name="gradient",
    )(saved_modes, mode_gains)


def solution(mesh):
    in_specs = (P("freq", None, None, None, None, "space", None, None), P("freq", None))
    out_specs = P("space", "freq", None)
    return jax.shard_map(local, mesh=mesh, in_specs=in_specs, out_specs=out_specs, check_vma=False)
```
